1024 devices in a mesh: orb: 32 (over z_hi, y, core), grp: 32 (over x, z_lo).
Axes of the slice: x: 8, y: 8, z: 8 (z_hi: 2, z_lo: 4; z = z_hi * 4 + z_lo), core: 2. Of those that a mesh axis runs over, the one named last changes fastest.
Arguments:
- targets: bfloat16 [32, 98304], P('orb'), may hold values from -6 to 6
- partners: bfloat16 [2048, 98304], P(('orb', 'grp')), may hold values from -24 to 24
Outputs:
- exchange: float32 [32, 98304], P('orb', 'grp')
The draws below stay inside these ranges and needn't reach their ends.
All inputs are finite; a program needn't handle non-finite values.
Results may differ from the reference program's by a relative error of at most 0.007.
Values may be sent and summed in bfloat16 or wider, within the bound.
No kernel may reach another device: no remote copies, remote signals or barrier semaphores. Data moves between devices by JAX's collectives and lax.ppermute only.
A program may use at most 32 MiB of HBM per device.

```python
import math
import jax
import jax.numpy as jnp
from jax import lax

X = 32
Y = 48
Z = 64
TGT = 1
PTN = 2
STEPS = 3
CELLS = 98304
TRIALS = 32
PARTNERS = 2048
N_ORB = 32
N_GRP = 32


def raised(values, rng, source, target, parts, factor):
    def block_of(axis_at):
        return (jnp.arange(values.shape[axis_at]) // (values.shape[axis_at] // parts)).reshape((-1,) + (1,) * (values.ndim - 1 - axis_at))

    first = jax.random.permutation(rng, parts)[block_of(target)]
    second = (block_of(target) + parts // 2) % parts
    return jnp.where((block_of(source) == first) | (block_of(source) == second), factor * values, values)


def levels(key, shape, split, low, largest):
    gain, own = 1.0, jax.random.fold_in(key, 6)
    for dim, parts in split:
        steps = jnp.exp(jax.random.uniform(jax.random.fold_in(own, dim), (parts,), jnp.float32, low / len(split), largest / len(split)))
        gain = gain * jnp.repeat(steps, shape[dim] // parts).reshape([-1 if axis == dim else 1 for axis in range(len(shape))])
    return gain


def normal_values(stream_key, shape, width, reach, pieces=(), kind=jnp.bfloat16):
    drawn = jax.random.normal(stream_key, shape, jnp.float32) * width
    if len(pieces) > 0:
        drawn = levels(stream_key, shape, pieces, -0.22, 0.18) * drawn
    return jnp.clip(drawn, min=-reach, max=reach).astype(kind)


def noise_with(stream_key, extent, width, limit, cuts, heavy, kind=jnp.bfloat16):
    array = width * jax.random.normal(stream_key, extent, jnp.float32)
    if cuts:
        array = array * levels(stream_key, extent, cuts, -0.22, 0.18)
    return jnp.clip(raised(array, jax.random.fold_in(stream_key, 3), *heavy), -limit, limit).astype(kind)


def setup_inputs(seed: int = 0) -> dict:
    key_of = jax.random.split(jax.random.key(seed), 3)
    return {
        "targets": normal_values(key_of[0], (TRIALS, CELLS), 1.0, 6.0, ((0, 32),)),
        "partners": noise_with(key_of[1], (PARTNERS, CELLS), 1.0, 24.0, ((0, 1024),), (0, 1, 1024, 6.0)),
    }


screening = 0.11
spacing = 0.45

def hartley(length):
    indices = jnp.arange(length, dtype=jnp.int32)
    product = indices[:, None] * indices[None, :] % length
    angles = 2.0 * math.pi / length * product.astype(jnp.float32)
    return (jnp.cos(angles) + jnp.sin(angles)).astype(jnp.bfloat16)

def squared_wave(length):
    indices = jnp.arange(length, dtype=jnp.int32)
    folded = jnp.minimum(indices, length - indices).astype(jnp.float32)
    wavenumber = 2.0 * math.pi / (length * spacing) * folded
    return wavenumber * wavenumber

def coulomb_table():
    squares = squared_wave(X)[:, None, None] + squared_wave(Y)[None, :, None] + squared_wave(Z)[None, None, :]
    positive = squares > 0.0
    guarded = jnp.where(positive, squares, 1.0)
    screened = 4.0 * math.pi * (1.0 - jnp.exp(-guarded / (4.0 * screening * screening))) / guarded
    kernel = jnp.where(positive, screened, math.pi / (screening * screening))
    spread = jnp.sqrt(jnp.mean(kernel * kernel))
    return kernel / (spread * (X * Y * Z))

def along(field, table, form):
    return jnp.einsum(form, field.astype(jnp.float32), table.astype(jnp.float32)).astype(jnp.bfloat16)

def pair_terms(target_rows, partner_rows, tables):
    table_x, table_y, table_z, kernel = tables
    target_grid = target_rows.reshape(TGT, 1, X, Y, Z).astype(jnp.float32)
    partner_grid = partner_rows.reshape(1, PTN, X, Y, Z).astype(jnp.float32)
    density = (target_grid * partner_grid).astype(jnp.bfloat16)
    density = along(density, table_z, 'tpxyz,wz->tpxyw')
    density = along(density, table_x, 'tpxyz,wx->tpwyz')
    density = along(density, table_y, 'tpxyz,wy->tpxwz')
    scaled = (density.astype(jnp.float32) * kernel).astype(jnp.bfloat16)
    scaled = along(scaled, table_z, 'tpxyz,wz->tpxyw')
    scaled = along(scaled, table_y, 'tpxyz,wy->tpxwz')
    scaled = along(scaled, table_x, 'tpxyz,wx->tpwyz')
    return lax.optimization_barrier(jnp.sum(scaled.astype(jnp.float32) * partner_grid, axis=1))

def reference(targets, partners):
    tables = (hartley(X), hartley(Y), hartley(Z), coulomb_table())
    cell_count = X * Y * Z
    target_blocks = targets.reshape(N_ORB, TGT, cell_count)
    partner_blocks = partners.reshape(N_ORB, N_GRP, PTN, cell_count)
    factor = 1.0 / math.sqrt(STEPS * N_GRP * PTN)

    def one_block(inputs):
        block_index, target_rows = inputs
        chosen = [lax.dynamic_index_in_dim(partner_blocks, ((block_index - step_index) % N_ORB).astype(jnp.int32), 0, keepdims=False) for step_index in range(STEPS)]
        group_sets = jnp.stack(chosen, axis=1)

        def one_group(running, partner_steps):
            partial_value = jnp.zeros((TGT, X, Y, Z), jnp.float32)
            for step_index in range(STEPS):
                partial_value = partial_value + pair_terms(target_rows, partner_steps[step_index], tables)
            return (running + partial_value, None)
        running, unused = lax.scan(one_group, jnp.zeros((TGT, X, Y, Z), jnp.float32), group_sets)
        return (-running * factor).reshape(TGT, cell_count)
    result = lax.map(one_block, (jnp.arange(N_ORB, dtype=jnp.int32), target_blocks))
    return result.reshape(N_ORB * TGT, cell_count)
```

```python
import functools
import math

import jax
import jax.numpy as jnp
import numpy as np
from jax import lax
from jax.experimental import pallas as pl
from jax.experimental.pallas import tpu as pltpu
from jax.sharding import PartitionSpec as P

X = 32
Y = 48
Z = 64
HALF = Y // 2
STEPS = 3
XB = 4
ROWS = XB * Y
GROUPS = X // XB

screening = 0.11
spacing = 0.45

bf16 = jnp.bfloat16
f32 = jnp.float32


def hartley(length):
    indices = np.arange(length)
    angles = 2.0 * np.pi / length * (indices[:, None] * indices[None, :] % length)
    return (np.cos(angles) + np.sin(angles)).astype(np.float32)


def squared_wave(length):
    indices = np.arange(length)
    folded = np.minimum(indices, length - indices)
    return (2.0 * np.pi / (length * spacing) * folded) ** 2


def coulomb_table():
    squares = (
        squared_wave(X)[:, None, None]
        + squared_wave(Y)[None, :, None]
        + squared_wave(Z)[None, None, :]
    )
    positive = squares > 0.0
    guarded = np.where(positive, squares, 1.0)
    screened = 4.0 * np.pi * (1.0 - np.exp(-guarded / (4.0 * screening * screening))) / guarded
    kernel = np.where(positive, screened, np.pi / (screening * screening))
    spread = np.sqrt(np.mean(kernel * kernel))
    return (kernel / (spread * (X * Y * Z))).astype(np.float32)


def tables():
    order = 2 * (np.arange(Y) % HALF) + np.arange(Y) // HALF
    along_y = hartley(Y)[:, order]
    as_bf16 = lambda t: jnp.asarray(t.astype(bf16))
    z4 = as_bf16(np.kron(np.eye(4, dtype=np.float32), hartley(Z)))
    y_in = as_bf16(np.kron(np.eye(XB, dtype=np.float32), along_y))
    y_out = as_bf16(np.kron(np.eye(XB, dtype=np.float32), along_y.T))
    x8 = as_bf16(np.kron(hartley(X), np.eye(8, dtype=np.float32)))
    kernel = jnp.asarray(np.tile(coulomb_table(), (1, 1, 2)))
    return z4, y_in, y_out, x8, kernel


def low_half(shape):
    return lax.broadcasted_iota(jnp.int32, shape, len(shape) - 1) < Z


def spread_rows(first, second):
    first = first.astype(f32).reshape(XB, HALF, 2 * Z)
    second = second.astype(f32).reshape(XB, HALF, 2 * Z)
    low = low_half(first.shape)
    even = jnp.where(low, first, pltpu.roll(second, Z, 2))
    odd = jnp.where(low, pltpu.roll(first, Z, 2), second)
    return jnp.concatenate([even, odd], axis=1).reshape(ROWS, 2 * Z).astype(bf16)


def gather_rows(field):
    planes = field.reshape(XB, Y, 2 * Z)
    planes = planes + pltpu.roll(planes, Z, 2)
    even, odd = planes[:, :HALF], planes[:, HALF:]
    return jnp.where(low_half(even.shape), even, odd)


def dot(a, b):
    return jnp.dot(a, b, preferred_element_type=f32)


def middle(work, x8, kernel, lanes):
    for block in range(Y // 8):
        rows = slice(block * 8, block * 8 + 8)
        field = work[:, rows, :].reshape(X * 8, lanes).astype(bf16)
        scale = kernel[:, rows, :].reshape(X * 8, 2 * Z)
        scale = jnp.concatenate([scale] * (lanes // (2 * Z)), axis=1)
        field = dot(x8[...], field)
        field = dot(x8[...], (field * scale).astype(bf16))
        work[:, rows, :] = field.reshape(X, 8, lanes)


def own_kernel(t_ref, p_ref, z4, y_in, y_out, x8, kernel, o_ref, work, pairs):
    z2 = z4[: 2 * Z, : 2 * Z]

    def inward(step, carry):
        rows = pl.ds(pl.multiple_of(step * (XB * HALF), XB * HALF), XB * HALF)
        rows2 = pl.ds(pl.multiple_of(step * (XB * HALF) + X * HALF, XB * HALF), XB * HALF)
        trial = t_ref[rows, :]
        trial = spread_rows(trial, trial)
        partner = spread_rows(p_ref[rows, :], p_ref[rows2, :])
        planes = pl.ds(step * XB, XB)
        pairs[pl.ds(pl.multiple_of(step * ROWS, ROWS), ROWS), :] = partner
        field = dot(trial * partner, z2).astype(bf16)
        work[planes] = dot(y_in[...], field).reshape(XB, Y, 2 * Z)
        return carry

    lax.fori_loop(0, GROUPS, inward, 0)
    middle(work, x8, kernel, 2 * Z)

    def outward(step, carry):
        planes = pl.ds(step * XB, XB)
        field = work[planes].reshape(ROWS, 2 * Z).astype(bf16)
        field = dot(y_out[...], field).astype(bf16)
        field = dot(field, z2)
        partner = pairs[pl.ds(pl.multiple_of(step * ROWS, ROWS), ROWS), :].astype(f32)
        o_ref[planes] = gather_rows(field * partner)
        return carry

    lax.fori_loop(0, GROUPS, outward, 0)


def cross_kernel(
    odd_ref, t_ref, r_ref, p_ref, q_ref, own_ref, z4, y_in, y_out, x8, kernel, o_ref, work, pairs
):
    odd = odd_ref[0] == 1

    def inward(step, carry):
        rows = pl.ds(pl.multiple_of(step * (XB * HALF), XB * HALF), XB * HALF)
        rows2 = pl.ds(pl.multiple_of(step * (XB * HALF) + X * HALF, XB * HALF), XB * HALF)
        remote = r_ref[rows, :]
        chosen = jnp.where(odd, t_ref[rows, :].astype(f32), remote.astype(f32))
        trial = jnp.concatenate(
            [spread_rows(remote, remote), spread_rows(chosen, chosen)], axis=1
        )
        partner = jnp.concatenate(
            [
                spread_rows(p_ref[rows, :], p_ref[rows2, :]),
                spread_rows(q_ref[rows, :], q_ref[rows2, :]),
            ],
            axis=1,
        )
        pairs[pl.ds(pl.multiple_of(step * ROWS, ROWS), ROWS), :] = partner
        field = dot(trial * partner, z4[...]).astype(bf16)
        work[pl.ds(step * XB, XB)] = dot(y_in[...], field).reshape(XB, Y, 4 * Z)
        return carry

    lax.fori_loop(0, GROUPS, inward, 0)
    middle(work, x8, kernel, 4 * Z)

    def outward(step, carry):
        planes = pl.ds(step * XB, XB)
        field = work[planes].reshape(ROWS, 4 * Z).astype(bf16)
        field = dot(y_out[...], field).astype(bf16)
        field = dot(field, z4[...])
        field = field * pairs[pl.ds(pl.multiple_of(step * ROWS, ROWS), ROWS), :].astype(f32)
        remote = gather_rows(field[:, : 2 * Z])
        chosen = gather_rows(field[:, 2 * Z :])
        own = own_ref[planes] + jnp.where(odd, chosen, 0.0)
        remote = remote + jnp.where(odd, 0.0, chosen)
        o_ref[planes] = jnp.concatenate([own, remote], axis=1).astype(bf16)
        return carry

    lax.fori_loop(0, GROUPS, outward, 0)


VMEM = pl.BlockSpec(memory_space=pltpu.VMEM)
SMEM = pl.BlockSpec(memory_space=pltpu.SMEM)


def own_call(target, partner, tabs):
    return pl.pallas_call(
        own_kernel,
        out_shape=jax.ShapeDtypeStruct((X, HALF, 2 * Z), f32),
        in_specs=[VMEM] * 7,
        out_specs=VMEM,
        scratch_shapes=[pltpu.VMEM((X, Y, 2 * Z), f32), pltpu.VMEM((X * Y, 2 * Z), bf16)],
        cost_estimate=pl.CostEstimate(flops=2 * 10**9, bytes_accessed=2 * 10**6, transcendentals=0),
        name="own_terms",
    )(target, partner, *tabs)


def cross_call(odd, target, remote, partner, other, own, tabs):
    return pl.pallas_call(
        cross_kernel,
        out_shape=jax.ShapeDtypeStruct((X, Y, 2 * Z), bf16),
        in_specs=[SMEM] + [VMEM] * 10,
        out_specs=VMEM,
        scratch_shapes=[pltpu.VMEM((X, Y, 4 * Z), f32), pltpu.VMEM((X * Y, 4 * Z), bf16)],
        cost_estimate=pl.CostEstimate(flops=4 * 10**9, bytes_accessed=3 * 10**6, transcendentals=0),
        name="cross_terms",
    )(odd, target, remote, partner, other, own, *tabs)


def trial_route(blocks, groups, high, low):
    half = blocks // high
    pairs = []
    for block in range(blocks):
        source = (block + 2) % blocks
        for group in range(groups):
            place = group % low
            if source // half != block // half:
                place = low - 1 - place
            pairs.append((source * groups + group // low * low + place, block * groups + group))
    return pairs


def local(targets, partners):
    blocks, groups = lax.axis_size("orb"), lax.axis_size("grp")
    target = targets.reshape(X * HALF, 2 * Z)
    remote = lax.ppermute(target, ("orb", "grp"), trial_route(blocks, groups, 2, 4))
    partner = partners.reshape(2 * X * HALF, 2 * Z)
    other = lax.ppermute(partner, "orb", [(i ^ 1, i) for i in range(blocks)])
    tabs = tables()
    odd = (lax.axis_index("orb") % 2).astype(jnp.int32).reshape(1)
    own = own_call(target, partner, tabs)
    fields = cross_call(odd, target, remote, partner, other, own, tabs)
    slabs = lax.all_to_all(fields, "grp", 0, 0, tiled=True)
    summed = jnp.sum(slabs.astype(f32), axis=0)
    ahead = lax.ppermute(summed[HALF:], "orb", [(i, (i + 2) % blocks) for i in range(blocks)])
    factor = -1.0 / math.sqrt(STEPS * groups * 2)
    return ((summed[:HALF] + ahead) * factor).reshape(1, Y * Z)


def solution(mesh):
    in_specs = (P("orb", None), P(("orb", "grp"), None))
    out_specs = P("orb", "grp")
    return jax.shard_map(local, mesh=mesh, in_specs=in_specs, out_specs=out_specs, check_vma=False)
```

```python
import math

import jax
import jax.numpy as jnp
import numpy as np
from jax import lax
from jax.experimental import pallas as pl
from jax.experimental.pallas import tpu as pltpu
from jax.sharding import PartitionSpec as P

X = 32
Y = 48
Z = 64
HALF = Y // 2
STEPS = 3
XB = 4
ROWS = XB * Y
GROUPS = X // XB

screening = 0.11
spacing = 0.45

bf16 = jnp.bfloat16
f32 = jnp.float32


def hartley(length):
    indices = np.arange(length)
    angles = 2.0 * np.pi / length * (indices[:, None] * indices[None, :] % length)
    return (np.cos(angles) + np.sin(angles)).astype(np.float32)


def squared_wave(length):
    indices = np.arange(length)
    folded = np.minimum(indices, length - indices)
    return (2.0 * np.pi / (length * spacing) * folded) ** 2


def coulomb_table():
    squares = (
        squared_wave(X)[:, None, None]
        + squared_wave(Y)[None, :, None]
        + squared_wave(Z)[None, None, :]
    )
    positive = squares > 0.0
    guarded = np.where(positive, squares, 1.0)
    screened = 4.0 * np.pi * (1.0 - np.exp(-guarded / (4.0 * screening * screening))) / guarded
    kernel = np.where(positive, screened, np.pi / (screening * screening))
    spread = np.sqrt(np.mean(kernel * kernel))
    return (kernel / (spread * (X * Y * Z))).astype(np.float32)


def tables():
    order = 2 * (np.arange(Y) % HALF) + np.arange(Y) // HALF
    along_y = hartley(Y)[:, order]
    as_bf16 = lambda t: jnp.asarray(t.astype(bf16))
    z4 = as_bf16(np.kron(np.eye(4, dtype=np.float32), hartley(Z)))
    y_in = as_bf16(np.kron(np.eye(XB, dtype=np.float32), along_y))
    y_out = as_bf16(np.kron(np.eye(XB, dtype=np.float32), along_y.T))
    x8 = as_bf16(np.kron(hartley(X), np.eye(8, dtype=np.float32)))
    kernel = jnp.asarray(np.tile(coulomb_table(), (1, 1, 2)))
    return z4, y_in, y_out, x8, kernel


def low_half(shape):
    return lax.broadcasted_iota(jnp.int32, shape, len(shape) - 1) < Z


def spread_rows(first, second):
    first = first.astype(f32).reshape(XB, HALF, 2 * Z)
    second = second.astype(f32).reshape(XB, HALF, 2 * Z)
    low = low_half(first.shape)
    even = jnp.where(low, first, pltpu.roll(second, Z, 2))
    odd = jnp.where(low, pltpu.roll(first, Z, 2), second)
    return jnp.concatenate([even, odd], axis=1).reshape(ROWS, 2 * Z).astype(bf16)


def gather_rows(field):
    planes = field.reshape(XB, Y, 2 * Z)
    planes = planes + pltpu.roll(planes, Z, 2)
    even, odd = planes[:, :HALF], planes[:, HALF:]
    return jnp.where(low_half(even.shape), even, odd)


def dot(a, b):
    return jnp.dot(a, b, preferred_element_type=f32)


def middle(work, x8, kernel, lanes):
    for block in range(Y // 8):
        rows = slice(block * 8, block * 8 + 8)
        field = work[:, rows, :].reshape(X * 8, lanes).astype(bf16)
        scale = kernel[:, rows, :].reshape(X * 8, 2 * Z)
        scale = jnp.concatenate([scale] * (lanes // (2 * Z)), axis=1)
        field = dot(x8[...], field)
        field = dot(x8[...], (field * scale).astype(bf16))
        work[:, rows, :] = field.reshape(X, 8, lanes)


def own_kernel(t_ref, p_ref, z4, y_in, y_out, x8, kernel, o_ref, work, pairs):
    z2 = z4[: 2 * Z, : 2 * Z]

    def inward(step, carry):
        rows = pl.ds(pl.multiple_of(step * (XB * HALF), XB * HALF), XB * HALF)
        rows2 = pl.ds(pl.multiple_of(step * (XB * HALF) + X * HALF, XB * HALF), XB * HALF)
        trial = t_ref[rows, :]
        trial = spread_rows(trial, trial)
        partner = spread_rows(p_ref[rows, :], p_ref[rows2, :])
        planes = pl.ds(step * XB, XB)
        pairs[pl.ds(pl.multiple_of(step * ROWS, ROWS), ROWS), :] = partner
        field = dot(trial * partner, z2).astype(bf16)
        work[planes] = dot(y_in[...], field).reshape(XB, Y, 2 * Z)
        return carry

    lax.fori_loop(0, GROUPS, inward, 0, unroll=GROUPS)
    middle(work, x8, kernel, 2 * Z)

    def outward(step, carry):
        planes = pl.ds(step * XB, XB)
        field = work[planes].reshape(ROWS, 2 * Z).astype(bf16)
        field = dot(y_out[...], field).astype(bf16)
        field = dot(field, z2)
        partner = pairs[pl.ds(pl.multiple_of(step * ROWS, ROWS), ROWS), :].astype(f32)
        o_ref[planes] = gather_rows(field * partner)
        return carry

    lax.fori_loop(0, GROUPS, outward, 0, unroll=GROUPS)


def cross_kernel(
    odd_ref, t_ref, r_ref, p_ref, q_ref, own_ref, z4, y_in, y_out, x8, kernel, o_ref, work, pairs
):
    odd = odd_ref[0] == 1

    def inward(step, carry):
        rows = pl.ds(pl.multiple_of(step * (XB * HALF), XB * HALF), XB * HALF)
        rows2 = pl.ds(pl.multiple_of(step * (XB * HALF) + X * HALF, XB * HALF), XB * HALF)
        remote = r_ref[rows, :]
        chosen = jnp.where(odd, t_ref[rows, :].astype(f32), remote.astype(f32))
        trial = jnp.concatenate(
            [spread_rows(remote, remote), spread_rows(chosen, chosen)], axis=1
        )
        partner = jnp.concatenate(
            [
                spread_rows(p_ref[rows, :], p_ref[rows2, :]),
                spread_rows(q_ref[rows, :], q_ref[rows2, :]),
            ],
            axis=1,
        )
        pairs[pl.ds(pl.multiple_of(step * ROWS, ROWS), ROWS), :] = partner
        field = dot(trial * partner, z4[...]).astype(bf16)
        work[pl.ds(step * XB, XB)] = dot(y_in[...], field).reshape(XB, Y, 4 * Z)
        return carry

    lax.fori_loop(0, GROUPS, inward, 0, unroll=GROUPS)
    middle(work, x8, kernel, 4 * Z)

    def outward(step, carry):
        planes = pl.ds(step * XB, XB)
        field = work[planes].reshape(ROWS, 4 * Z).astype(bf16)
        field = dot(y_out[...], field).astype(bf16)
        field = dot(field, z4[...])
        field = field * pairs[pl.ds(pl.multiple_of(step * ROWS, ROWS), ROWS), :].astype(f32)
        remote = gather_rows(field[:, : 2 * Z])
        chosen = gather_rows(field[:, 2 * Z :])
        own = own_ref[planes] + jnp.where(odd, chosen, 0.0)
        remote = remote + jnp.where(odd, 0.0, chosen)
        o_ref[planes] = jnp.concatenate([own, remote], axis=1).astype(bf16)
        return carry

    lax.fori_loop(0, GROUPS, outward, 0, unroll=GROUPS)


VMEM = pl.BlockSpec(memory_space=pltpu.VMEM)
SMEM = pl.BlockSpec(memory_space=pltpu.SMEM)


def own_call(target, partner, tabs):
    return pl.pallas_call(
        own_kernel,
        out_shape=jax.ShapeDtypeStruct((X, HALF, 2 * Z), f32),
        in_specs=[VMEM] * 7,
        out_specs=VMEM,
        scratch_shapes=[pltpu.VMEM((X, Y, 2 * Z), f32), pltpu.VMEM((X * Y, 2 * Z), bf16)],
        cost_estimate=pl.CostEstimate(flops=2 * 10**9, bytes_accessed=2 * 10**6, transcendentals=0),
        compiler_params=pltpu.CompilerParams(vmem_limit_bytes=16 * 2**20),
        name="own_terms",
    )(target, partner, *tabs)


def cross_call(odd, target, remote, partner, other, own, tabs):
    return pl.pallas_call(
        cross_kernel,
        out_shape=jax.ShapeDtypeStruct((X, Y, 2 * Z), bf16),
        in_specs=[SMEM] + [VMEM] * 10,
        out_specs=VMEM,
        scratch_shapes=[pltpu.VMEM((X, Y, 4 * Z), f32), pltpu.VMEM((X * Y, 4 * Z), bf16)],
        cost_estimate=pl.CostEstimate(flops=4 * 10**9, bytes_accessed=3 * 10**6, transcendentals=0),
        compiler_params=pltpu.CompilerParams(vmem_limit_bytes=16 * 2**20),
        name="cross_terms",
    )(odd, target, remote, partner, other, own, *tabs)


LOW = 4


def trial_route(blocks, groups):
    half = blocks // 2
    pairs = []
    for block in range(blocks):
        source = (block + 2) % blocks
        for group in range(groups):
            mirror = group // LOW * LOW + LOW - 1 - group % LOW
            place = mirror if source // half != block // half else group
            pairs.append((source * groups + place, block * groups + group))
    return pairs


def local(targets, partners):
    blocks, groups = lax.axis_size("orb"), lax.axis_size("grp")
    block = lax.axis_index("orb")
    target = targets.reshape(X * HALF, 2 * Z)
    remote = lax.ppermute(target, ("orb", "grp"), trial_route(blocks, groups))
    partner = partners.reshape(2 * X * HALF, 2 * Z)
    other = lax.ppermute(partner, "orb", [(i ^ 1, i) for i in range(blocks)])
    tabs = tables()
    odd = (block % 2).astype(jnp.int32).reshape(1)
    own = own_call(target, partner, tabs)
    fields = cross_call(odd, target, remote, partner, other, own, tabs)
    slabs = lax.all_to_all(fields, "grp", 0, 0, tiled=True)
    summed = jnp.sum(slabs.astype(f32), axis=0)
    ahead = lax.ppermute(summed[HALF:], "orb", [(i, (i + 2) % blocks) for i in range(blocks)])
    factor = -1.0 / math.sqrt(STEPS * groups * 2)
    return ((summed[:HALF] + ahead) * factor).reshape(1, Y * Z)


def solution(mesh):
    in_specs = (P("orb", None), P(("orb", "grp"), None))
    out_specs = P("orb", "grp")
    return jax.shard_map(local, mesh=mesh, in_specs=in_specs, out_specs=out_specs, check_vma=False)
```

```python
import math

import jax
import jax.numpy as jnp
import numpy as np
from jax import lax
from jax.experimental import pallas as pl
from jax.experimental.pallas import tpu as pltpu
from jax.sharding import PartitionSpec as P

X = 32
Y = 48
Z = 64
HALF = Y // 2
STEPS = 3
XB = 4
ROWS = XB * Y
GROUPS = X // XB
SIDE = 256

screening = 0.11
spacing = 0.45

bf16 = jnp.bfloat16
f32 = jnp.float32


def hartley(length):
    indices = np.arange(length)
    angles = 2.0 * np.pi / length * (indices[:, None] * indices[None, :] % length)
    return (np.cos(angles) + np.sin(angles)).astype(np.float32)


def squared_wave(length):
    indices = np.arange(length)
    folded = np.minimum(indices, length - indices)
    return (2.0 * np.pi / (length * spacing) * folded) ** 2


def coulomb_table():
    squares = (
        squared_wave(X)[:, None, None]
        + squared_wave(Y)[None, :, None]
        + squared_wave(Z)[None, None, :]
    )
    positive = squares > 0.0
    guarded = np.where(positive, squares, 1.0)
    screened = 4.0 * np.pi * (1.0 - np.exp(-guarded / (4.0 * screening * screening))) / guarded
    kernel = np.where(positive, screened, np.pi / (screening * screening))
    spread = np.sqrt(np.mean(kernel * kernel))
    return (kernel / (spread * (X * Y * Z))).astype(np.float32)


def tables():
    order = 2 * (np.arange(Y) % HALF) + np.arange(Y) // HALF
    along_y = hartley(Y)[:, order]
    joined = np.zeros((SIDE, 4 * SIDE), np.float32)
    joined[:, :SIDE] = np.kron(np.eye(4, dtype=np.float32), hartley(Z))
    joined[:, SIDE : 2 * SIDE] = np.kron(hartley(X), np.eye(8, dtype=np.float32))
    joined[:ROWS, 2 * SIDE : 2 * SIDE + ROWS] = np.kron(np.eye(XB, dtype=np.float32), along_y)
    joined[:ROWS, 3 * SIDE : 3 * SIDE + ROWS] = np.kron(np.eye(XB, dtype=np.float32), along_y.T)
    kernel = jnp.asarray(np.tile(coulomb_table(), (1, 1, 2)))
    return jnp.asarray(joined.astype(bf16)), kernel


def views(joined):
    return (
        joined.at[:, :SIDE],
        joined.at[:, SIDE : 2 * SIDE],
        joined.at[:ROWS, 2 * SIDE : 2 * SIDE + ROWS],
        joined.at[:ROWS, 3 * SIDE : 3 * SIDE + ROWS],
    )


def low_half(shape):
    return lax.broadcasted_iota(jnp.int32, shape, len(shape) - 1) < Z


def spread_rows(first, second):
    first = first.astype(f32).reshape(XB, HALF, 2 * Z)
    second = second.astype(f32).reshape(XB, HALF, 2 * Z)
    low = low_half(first.shape)
    even = jnp.where(low, first, pltpu.roll(second, Z, 2))
    odd = jnp.where(low, pltpu.roll(first, Z, 2), second)
    return jnp.concatenate([even, odd], axis=1).reshape(ROWS, 2 * Z).astype(bf16)


def gather_rows(field):
    planes = field.reshape(XB, Y, 2 * Z)
    planes = planes + pltpu.roll(planes, Z, 2)
    even, odd = planes[:, :HALF], planes[:, HALF:]
    return jnp.where(low_half(even.shape), even, odd)


def dot(a, b):
    return jnp.dot(a, b, preferred_element_type=f32)


def middle(work, x8, kernel, lanes):
    for block in range(Y // 8):
        rows = slice(block * 8, block * 8 + 8)
        field = work[:, rows, :].reshape(X * 8, lanes).astype(bf16)
        scale = kernel[:, rows, :].reshape(X * 8, 2 * Z)
        scale = jnp.concatenate([scale] * (lanes // (2 * Z)), axis=1)
        field = dot(x8[...], field)
        field = dot(x8[...], (field * scale).astype(bf16))
        work[:, rows, :] = field.reshape(X, 8, lanes)


def chunk(step, high, base=0):
    return pl.ds(pl.multiple_of(step * high + base, high), high)


def density(trial, partner):
    trial = spread_rows(trial, trial)
    return jnp.concatenate([trial * partner[:, : 2 * Z], trial * partner[:, 2 * Z :]], axis=1)


def inward(field, z4, y_in):
    return dot(y_in[...], dot(field, z4[...]).astype(bf16)).reshape(XB, Y, 4 * Z)


def outward(work, step, partner, both, z4, y_out):
    field = work[pl.ds(step * XB, XB)].reshape(ROWS, 4 * Z).astype(bf16)
    field = dot(dot(y_out[...], field).astype(bf16), z4[...]) * partner.astype(f32)
    return gather_rows(field[:, : 2 * Z] + jnp.where(both, field[:, 2 * Z :], 0.0))


def own_kernel(
    odd_ref, t_ref, p_ref, q_ref, joined, kernel, o_ref, pairs, work
):
    z4, x8, y_in, y_out = views(joined)
    odd = odd_ref[0] == 1
    high = XB * HALF
    for step in range(GROUPS):
        rows, rows2 = chunk(step, high), chunk(step, high, X * HALF)
        partner = jnp.concatenate(
            [
                spread_rows(p_ref[rows, :], p_ref[rows2, :]),
                spread_rows(q_ref[rows, :], q_ref[rows2, :]),
            ],
            axis=1,
        )
        pairs[chunk(step, ROWS), :] = partner
        work[pl.ds(step * XB, XB)] = inward(density(t_ref[rows, :], partner), z4, y_in)
    middle(work, x8, kernel, 4 * Z)
    for step in range(GROUPS):
        partner = pairs[chunk(step, ROWS), :]
        o_ref[pl.ds(step * XB, XB)] = outward(work, step, partner, odd, z4, y_out)


def cross_kernel(
    odd_ref, t_ref, pairs, own_ref, joined, kernel, o_ref, work
):
    z4, x8, y_in, y_out = views(joined)
    even = odd_ref[0] == 0
    for step in range(GROUPS):
        partner = pairs[chunk(step, ROWS), :]
        field = density(t_ref[chunk(step, XB * HALF), :], partner)
        work[pl.ds(step * XB, XB)] = inward(field, z4, y_in)
    middle(work, x8, kernel, 4 * Z)
    for step in range(GROUPS):
        partner = pairs[chunk(step, ROWS), :]
        cross = outward(work, step, partner, even, z4, y_out)
        planes = pl.ds(step * XB, XB)
        o_ref[planes] = jnp.concatenate([own_ref[planes], cross], axis=1).astype(bf16)


def rows_kernel(x_ref, o_ref):
    o_ref[...] = x_ref[...].reshape(o_ref.shape)


PARTS = 4


def split_rows_kernel(x_ref, o_ref, landed, sems):
    width = x_ref.shape[1] // PARTS
    high = o_ref.shape[0] // PARTS
    copies = []
    for part in range(PARTS):
        columns = slice(part * width, (part + 1) * width)
        copies.append(
            pltpu.make_async_copy(x_ref.at[:, columns], landed.at[:, columns], sems.at[part])
        )
        copies[-1].start()
    for part, copy in enumerate(copies):
        copy.wait()
        field = landed[:, part * width : (part + 1) * width]
        o_ref[part * high : (part + 1) * high, :] = field.reshape(high, 2 * Z)


VMEM = pl.BlockSpec(memory_space=pltpu.VMEM)
SMEM = pl.BlockSpec(memory_space=pltpu.SMEM)
GRANT = pltpu.CompilerParams(vmem_limit_bytes=16 * 2**20)


def as_rows(fields):
    return pl.pallas_call(
        rows_kernel,
        out_shape=jax.ShapeDtypeStruct((fields.shape[0] * X * HALF, 2 * Z), bf16),
        in_specs=[VMEM],
        out_specs=VMEM,
        cost_estimate=pl.CostEstimate(flops=0, bytes_accessed=10**6, transcendentals=0),
        compiler_params=GRANT,
        name="as_rows",
    )(fields)


def as_rows_early(fields):
    return pl.pallas_call(
        split_rows_kernel,
        out_shape=jax.ShapeDtypeStruct((fields.shape[0] * X * HALF, 2 * Z), bf16),
        in_specs=[pl.BlockSpec(memory_space=pltpu.HBM)],
        out_specs=VMEM,
        scratch_shapes=[pltpu.VMEM(fields.shape, bf16), pltpu.SemaphoreType.DMA((PARTS,))],
        cost_estimate=pl.CostEstimate(flops=0, bytes_accessed=10**6, transcendentals=0),
        compiler_params=GRANT,
        name="as_rows_early",
    )(fields)


COST = pl.CostEstimate(flops=4 * 10**9, bytes_accessed=3 * 10**6, transcendentals=0)
WORK = pltpu.VMEM((X, Y, 4 * Z), f32)


def own_call(odd, trial, partner, other, tabs):
    return pl.pallas_call(
        own_kernel,
        out_shape=(
            jax.ShapeDtypeStruct((X, HALF, 2 * Z), f32),
            jax.ShapeDtypeStruct((X * Y, 4 * Z), bf16),
        ),
        in_specs=[SMEM] + [VMEM] * 5,
        out_specs=(VMEM, VMEM),
        scratch_shapes=[WORK],
        cost_estimate=COST,
        compiler_params=GRANT,
        name="own_terms",
    )(odd, trial, partner, other, *tabs)


def cross_call(odd, trial, pairs, own, tabs):
    return pl.pallas_call(
        cross_kernel,
        out_shape=jax.ShapeDtypeStruct((X, Y, 2 * Z), bf16),
        in_specs=[SMEM] + [VMEM] * 5,
        out_specs=VMEM,
        scratch_shapes=[WORK],
        cost_estimate=COST,
        compiler_params=GRANT,
        name="cross_terms",
    )(odd, trial, pairs, own, *tabs)


LOW = 4


def trial_route(blocks, groups):
    half = blocks // 2
    pairs = []
    for block in range(blocks):
        source = (block + 2) % blocks
        for group in range(groups):
            place = group % LOW
            if source // half != block // half:
                if block % 2 == 0:
                    place = LOW - 1 - place
                else:
                    place = (place + (1 if block >= half else LOW - 1)) % LOW
            pairs.append((source * groups + group // LOW * LOW + place, block * groups + group))
    return pairs


def local(targets, partners):
    blocks, groups = lax.axis_size("orb"), lax.axis_size("grp")
    block = lax.axis_index("orb")
    target = as_rows_early(targets)
    remote = lax.ppermute(target, ("orb", "grp"), trial_route(blocks, groups))
    partner = as_rows(partners)
    other = lax.ppermute(partner, "orb", [(i ^ 1, i) for i in range(blocks)])
    tabs = tables()
    odd = (block % 2).astype(jnp.int32).reshape(1)
    own, pairs = own_call(odd, target, partner, other, tabs)
    fields = cross_call(odd, remote, pairs, own, tabs)
    slabs = lax.all_to_all(fields, "grp", 0, 0, tiled=True)
    summed = jnp.sum(slabs.astype(f32), axis=0)
    ahead = lax.ppermute(summed[HALF:], "orb", [(i, (i + 2) % blocks) for i in range(blocks)])
    factor = -1.0 / math.sqrt(STEPS * groups * 2)
    return ((summed[:HALF] + ahead) * factor).reshape(1, Y * Z)


def solution(mesh):
    in_specs = (P("orb", None), P(("orb", "grp"), None))
    out_specs = P("orb", "grp")
    return jax.shard_map(local, mesh=mesh, in_specs=in_specs, out_specs=out_specs, check_vma=False)
```

```python
import math

import jax
import jax.numpy as jnp
import numpy as np
from jax import lax
from jax.experimental import pallas as pl
from jax.experimental.pallas import tpu as pltpu
from jax.sharding import PartitionSpec as P

X = 32
Y = 48
Z = 64
HALF = Y // 2
STEPS = 3
XB = 4
ROWS = XB * Y
GROUPS = X // XB
SIDE = 256

screening = 0.11
spacing = 0.45

bf16 = jnp.bfloat16
f32 = jnp.float32


def hartley(length):
    indices = np.arange(length)
    angles = 2.0 * np.pi / length * (indices[:, None] * indices[None, :] % length)
    return (np.cos(angles) + np.sin(angles)).astype(np.float32)


def squared_wave(length):
    indices = np.arange(length)
    folded = np.minimum(indices, length - indices)
    return (2.0 * np.pi / (length * spacing) * folded) ** 2


def coulomb_table():
    squares = (
        squared_wave(X)[:, None, None]
        + squared_wave(Y)[None, :, None]
        + squared_wave(Z)[None, None, :]
    )
    positive = squares > 0.0
    guarded = np.where(positive, squares, 1.0)
    screened = 4.0 * np.pi * (1.0 - np.exp(-guarded / (4.0 * screening * screening))) / guarded
    kernel = np.where(positive, screened, np.pi / (screening * screening))
    spread = np.sqrt(np.mean(kernel * kernel))
    return (kernel / (spread * (X * Y * Z))).astype(np.float32)


def tables():
    order = 2 * (np.arange(Y) % HALF) + np.arange(Y) // HALF
    along_y = hartley(Y)[:, order]
    joined = np.zeros((SIDE, 4 * SIDE), np.float32)
    joined[:, :SIDE] = np.kron(np.eye(4, dtype=np.float32), hartley(Z))
    joined[:, SIDE : 2 * SIDE] = np.kron(hartley(X), np.eye(8, dtype=np.float32))
    joined[:ROWS, 2 * SIDE : 2 * SIDE + ROWS] = np.kron(np.eye(XB, dtype=np.float32), along_y)
    joined[:ROWS, 3 * SIDE : 3 * SIDE + ROWS] = np.kron(np.eye(XB, dtype=np.float32), along_y.T)
    kernel = jnp.asarray(np.tile(coulomb_table(), (1, 1, 2)))
    return jnp.asarray(joined.astype(bf16)), kernel


def views(joined):
    return (
        joined.at[:, :SIDE],
        joined.at[:, SIDE : 2 * SIDE],
        joined.at[:ROWS, 2 * SIDE : 2 * SIDE + ROWS],
        joined.at[:ROWS, 3 * SIDE : 3 * SIDE + ROWS],
    )


def low_half(shape):
    return lax.broadcasted_iota(jnp.int32, shape, len(shape) - 1) < Z


def spread_rows(first, second):
    first = first.astype(f32).reshape(XB, HALF, 2 * Z)
    second = second.astype(f32).reshape(XB, HALF, 2 * Z)
    low = low_half(first.shape)
    even = jnp.where(low, first, pltpu.roll(second, Z, 2))
    odd = jnp.where(low, pltpu.roll(first, Z, 2), second)
    return jnp.concatenate([even, odd], axis=1).reshape(ROWS, 2 * Z).astype(bf16)


def gather_rows(field):
    planes = field.reshape(XB, Y, 2 * Z)
    planes = planes + pltpu.roll(planes, Z, 2)
    even, odd = planes[:, :HALF], planes[:, HALF:]
    return jnp.where(low_half(even.shape), even, odd)


def dot(a, b):
    return jnp.dot(a, b, preferred_element_type=f32)


def middle(work, x8, kernel, lanes):
    for block in range(Y // 8):
        rows = slice(block * 8, block * 8 + 8)
        field = work[:, rows, :].reshape(X * 8, lanes).astype(bf16)
        scale = kernel[:, rows, :].reshape(X * 8, 2 * Z)
        scale = jnp.concatenate([scale] * (lanes // (2 * Z)), axis=1)
        field = dot(x8[...], field)
        field = dot(x8[...], (field * scale).astype(bf16))
        work[:, rows, :] = field.reshape(X, 8, lanes)


def chunk(step, high, base=0):
    return pl.ds(pl.multiple_of(step * high + base, high), high)


def density(trial, partner):
    trial = spread_rows(trial, trial)
    return jnp.concatenate([trial * partner[:, : 2 * Z], trial * partner[:, 2 * Z :]], axis=1)


def inward(field, z4, y_in):
    return dot(y_in[...], dot(field, z4[...]).astype(bf16)).reshape(XB, Y, 4 * Z)


def outward(work, step, partner, both, z4, y_out):
    field = work[pl.ds(step * XB, XB)].reshape(ROWS, 4 * Z).astype(bf16)
    field = dot(dot(y_out[...], field).astype(bf16), z4[...]) * partner.astype(f32)
    return gather_rows(field[:, : 2 * Z] + jnp.where(both, field[:, 2 * Z :], 0.0))


def own_kernel(flags_ref, t_ref, p_ref, q_ref, joined, kernel, o_ref, pairs, work):
    z4, x8, y_in, y_out = views(joined)
    odd = flags_ref[0] == 1
    high = XB * HALF
    for step in range(GROUPS):
        rows, rows2 = chunk(step, high), chunk(step, high, X * HALF)
        partner = jnp.concatenate(
            [
                spread_rows(p_ref[rows, :], p_ref[rows2, :]),
                spread_rows(q_ref[rows, :], q_ref[rows2, :]),
            ],
            axis=1,
        )
        pairs[chunk(step, ROWS), :] = partner
        work[pl.ds(step * XB, XB)] = inward(density(t_ref[rows, :], partner), z4, y_in)
    middle(work, x8, kernel, 4 * Z)
    for step in range(GROUPS):
        partner = pairs[chunk(step, ROWS), :]
        o_ref[pl.ds(step * XB, XB)] = outward(work, step, partner, odd, z4, y_out)


def cross_kernel(flags_ref, t_ref, pairs, own_ref, joined, kernel, o_ref, work):
    z4, x8, y_in, y_out = views(joined)
    even = flags_ref[0] == 0
    border = flags_ref[1] == 1
    for step in range(GROUPS):
        partner = pairs[chunk(step, ROWS), :]
        field = density(t_ref[chunk(step, XB * HALF), :], partner)
        work[pl.ds(step * XB, XB)] = inward(field, z4, y_in)
    middle(work, x8, kernel, 4 * Z)
    for step in range(GROUPS):
        partner = pairs[chunk(step, ROWS), :]
        cross = outward(work, step, partner, even, z4, y_out)
        turned = jnp.concatenate([cross[i : i + 1] for i in reversed(range(XB))], axis=0)
        cross = jnp.where(border, turned, cross)
        planes = pl.ds(step * XB, XB)
        o_ref[planes] = jnp.concatenate([own_ref[planes], cross], axis=1).astype(bf16)


def rows_kernel(x_ref, o_ref):
    o_ref[...] = x_ref[...].reshape(o_ref.shape)


VMEM = pl.BlockSpec(memory_space=pltpu.VMEM)
SMEM = pl.BlockSpec(memory_space=pltpu.SMEM)
GRANT = pltpu.CompilerParams(vmem_limit_bytes=16 * 2**20)


def as_rows(fields):
    return pl.pallas_call(
        rows_kernel,
        out_shape=jax.ShapeDtypeStruct((fields.shape[0] * X * HALF, 2 * Z), bf16),
        in_specs=[VMEM],
        out_specs=VMEM,
        cost_estimate=pl.CostEstimate(flops=0, bytes_accessed=10**6, transcendentals=0),
        compiler_params=GRANT,
        name="as_rows",
    )(fields)


COST = pl.CostEstimate(flops=4 * 10**9, bytes_accessed=3 * 10**6, transcendentals=0)
WORK = pltpu.VMEM((X, Y, 4 * Z), f32)


def own_call(flags, trial, partner, other, tabs):
    return pl.pallas_call(
        own_kernel,
        out_shape=(
            jax.ShapeDtypeStruct((X, HALF, 2 * Z), f32),
            jax.ShapeDtypeStruct((X * Y, 4 * Z), bf16),
        ),
        in_specs=[SMEM] + [VMEM] * 5,
        out_specs=(VMEM, VMEM),
        scratch_shapes=[WORK],
        cost_estimate=COST,
        compiler_params=GRANT,
        name="own_terms",
    )(flags, trial, partner, other, *tabs)


def cross_call(flags, trial, pairs, own, tabs):
    return pl.pallas_call(
        cross_kernel,
        out_shape=jax.ShapeDtypeStruct((X, Y, 2 * Z), bf16),
        in_specs=[SMEM] + [VMEM] * 5,
        out_specs=VMEM,
        scratch_shapes=[WORK],
        cost_estimate=COST,
        compiler_params=GRANT,
        name="cross_terms",
    )(flags, trial, pairs, own, *tabs)


LOW = 4


def trial_route(blocks, groups):
    half = blocks // 2
    pairs = []
    for block in range(blocks):
        source = (block + 2) % blocks
        for group in range(groups):
            place = group % LOW
            if source // half != block // half:
                if block % 2 == 0:
                    place = LOW - 1 - place
                else:
                    place = (place + (1 if block >= half else LOW - 1)) % LOW
            pairs.append((source * groups + group // LOW * LOW + place, block * groups + group))
    return pairs


def slab_route(blocks, groups):
    half = blocks // 2
    pairs = []
    for block in range(blocks):
        owner = (block + 2) % blocks
        for group in range(groups):
            mirror = group // LOW * LOW + LOW - 1 - group % LOW
            place = mirror if owner // half != block // half else group
            pairs.append((block * groups + group, owner * groups + place))
    return pairs


def local(targets, partners):
    blocks, groups = lax.axis_size("orb"), lax.axis_size("grp")
    block = lax.axis_index("orb")
    target = as_rows(targets)
    remote = lax.ppermute(target, ("orb", "grp"), trial_route(blocks, groups))
    partner = as_rows(partners)
    other = lax.ppermute(partner, "orb", [(i ^ 1, i) for i in range(blocks)])
    tabs = tables()
    half = blocks // 2
    flags = jnp.stack([block % 2, (block % half >= half - 2).astype(jnp.int32)])
    own, pairs = own_call(flags, target, partner, other, tabs)
    fields = cross_call(flags, remote, pairs, own, tabs)
    slabs = lax.all_to_all(fields, "grp", 0, 0, tiled=True)
    summed = jnp.sum(slabs.astype(f32), axis=0)
    ahead = lax.ppermute(summed[HALF:], ("orb", "grp"), slab_route(blocks, groups))
    factor = -1.0 / math.sqrt(STEPS * groups * 2)
    return ((summed[:HALF] + ahead) * factor).reshape(1, Y * Z)


def solution(mesh):
    in_specs = (P("orb", None), P(("orb", "grp"), None))
    out_specs = P("orb", "grp")
    return jax.shard_map(local, mesh=mesh, in_specs=in_specs, out_specs=out_specs, check_vma=False)
```

```python
import math

import jax
import jax.numpy as jnp
import numpy as np
from jax import lax
from jax.experimental import pallas as pl
from jax.experimental.pallas import tpu as pltpu
from jax.sharding import PartitionSpec as P

X = 32
Y = 48
Z = 64
HALF = Y // 2
STEPS = 3
XB = 4
ROWS = XB * Y
GROUPS = X // XB
SIDE = 256

screening = 0.11
spacing = 0.45

bf16 = jnp.bfloat16
f32 = jnp.float32


def hartley(length):
    indices = np.arange(length)
    angles = 2.0 * np.pi / length * (indices[:, None] * indices[None, :] % length)
    return (np.cos(angles) + np.sin(angles)).astype(np.float32)


def squared_wave(length):
    indices = np.arange(length)
    folded = np.minimum(indices, length - indices)
    return (2.0 * np.pi / (length * spacing) * folded) ** 2


def coulomb_table():
    squares = (
        squared_wave(X)[:, None, None]
        + squared_wave(Y)[None, :, None]
        + squared_wave(Z)[None, None, :]
    )
    positive = squares > 0.0
    guarded = np.where(positive, squares, 1.0)
    screened = 4.0 * np.pi * (1.0 - np.exp(-guarded / (4.0 * screening * screening))) / guarded
    kernel = np.where(positive, screened, np.pi / (screening * screening))
    spread = np.sqrt(np.mean(kernel * kernel))
    return (kernel / (spread * (X * Y * Z))).astype(np.float32)


def tables():
    order = 2 * (np.arange(Y) % HALF) + np.arange(Y) // HALF
    along_y = hartley(Y)[:, order]
    joined = np.zeros((SIDE, 4 * SIDE), np.float32)
    joined[:, :SIDE] = np.kron(np.eye(4, dtype=np.float32), hartley(Z))
    joined[:, SIDE : 2 * SIDE] = np.kron(hartley(X), np.eye(8, dtype=np.float32))
    joined[:ROWS, 2 * SIDE : 2 * SIDE + ROWS] = np.kron(np.eye(XB, dtype=np.float32), along_y)
    joined[:ROWS, 3 * SIDE : 3 * SIDE + ROWS] = np.kron(np.eye(XB, dtype=np.float32), along_y.T)
    kernel = jnp.asarray(np.tile(coulomb_table(), (1, 1, 2)))
    return jnp.asarray(joined.astype(bf16)), kernel


def views(joined):
    return (
        joined.at[:, :SIDE],
        joined.at[:, SIDE : 2 * SIDE],
        joined.at[:ROWS, 2 * SIDE : 2 * SIDE + ROWS],
        joined.at[:ROWS, 3 * SIDE : 3 * SIDE + ROWS],
    )


def low_half(shape):
    return lax.broadcasted_iota(jnp.int32, shape, len(shape) - 1) < Z


def spread_rows(first, second):
    first = first.astype(f32).reshape(XB, HALF, 2 * Z)
    second = second.astype(f32).reshape(XB, HALF, 2 * Z)
    low = low_half(first.shape)
    even = jnp.where(low, first, pltpu.roll(second, Z, 2))
    odd = jnp.where(low, pltpu.roll(first, Z, 2), second)
    return jnp.concatenate([even, odd], axis=1).reshape(ROWS, 2 * Z).astype(bf16)


def gather_rows(field):
    planes = field.reshape(XB, Y, 2 * Z)
    planes = planes + pltpu.roll(planes, Z, 2)
    even, odd = planes[:, :HALF], planes[:, HALF:]
    return jnp.where(low_half(even.shape), even, odd)


def dot(a, b):
    return jnp.dot(a, b, preferred_element_type=f32)


def middle(work, x8, kernel, lanes):
    for block in range(Y // 8):
        rows = slice(block * 8, block * 8 + 8)
        field = work[:, rows, :].reshape(X * 8, lanes).astype(bf16)
        scale = kernel[:, rows, :].reshape(X * 8, 2 * Z)
        scale = jnp.concatenate([scale] * (lanes // (2 * Z)), axis=1)
        field = dot(x8[...], field)
        field = dot(x8[...], (field * scale).astype(bf16))
        work[:, rows, :] = field.reshape(X, 8, lanes)


def chunk(step, high, base=0):
    return pl.ds(pl.multiple_of(step * high + base, high), high)


def density(trial, partner):
    trial = spread_rows(trial, trial)
    return jnp.concatenate([trial * partner[:, : 2 * Z], trial * partner[:, 2 * Z :]], axis=1)


def inward(field, z4, y_in):
    return dot(y_in[...], dot(field, z4[...]).astype(bf16)).reshape(XB, Y, 4 * Z)


def outward(work, step, partner, both, z4, y_out):
    field = work[pl.ds(step * XB, XB)].reshape(ROWS, 4 * Z).astype(bf16)
    field = dot(dot(y_out[...], field).astype(bf16), z4[...]) * partner.astype(f32)
    return gather_rows(field[:, : 2 * Z] + jnp.where(both, field[:, 2 * Z :], 0.0))


def own_kernel(t_ref, p_ref, q_ref, joined, kernel, o_ref, pairs, work):
    z4, x8, y_in, y_out = views(joined)
    odd = lax.axis_index("orb") % 2 == 1
    high = XB * HALF
    for step in range(GROUPS):
        rows, rows2 = chunk(step, high), chunk(step, high, X * HALF)
        partner = jnp.concatenate(
            [
                spread_rows(p_ref[rows, :], p_ref[rows2, :]),
                spread_rows(q_ref[rows, :], q_ref[rows2, :]),
            ],
            axis=1,
        )
        pairs[chunk(step, ROWS), :] = partner
        work[pl.ds(step * XB, XB)] = inward(density(t_ref[rows, :], partner), z4, y_in)
    middle(work, x8, kernel, 4 * Z)
    for step in range(GROUPS):
        partner = pairs[chunk(step, ROWS), :]
        o_ref[pl.ds(step * XB, XB)] = outward(work, step, partner, odd, z4, y_out)


def cross_kernel(t_ref, pairs, own_ref, joined, kernel, o_ref, work):
    z4, x8, y_in, y_out = views(joined)
    block = lax.axis_index("orb")
    half = lax.axis_size("orb") // 2
    even = block % 2 == 0
    border = block % half >= half - 2
    for step in range(GROUPS):
        partner = pairs[chunk(step, ROWS), :]
        field = density(t_ref[chunk(step, XB * HALF), :], partner)
        work[pl.ds(step * XB, XB)] = inward(field, z4, y_in)
    middle(work, x8, kernel, 4 * Z)
    for step in range(GROUPS):
        partner = pairs[chunk(step, ROWS), :]
        cross = outward(work, step, partner, even, z4, y_out)
        turned = jnp.concatenate([cross[i : i + 1] for i in reversed(range(XB))], axis=0)
        cross = jnp.where(border, turned, cross)
        planes = pl.ds(step * XB, XB)
        o_ref[planes] = jnp.concatenate([own_ref[planes], cross], axis=1).astype(bf16)


def rows_kernel(x_ref, o_ref):
    o_ref[...] = x_ref[...].reshape(o_ref.shape)


VMEM = pl.BlockSpec(memory_space=pltpu.VMEM)
GRANT = pltpu.CompilerParams(vmem_limit_bytes=16 * 2**20)


def as_rows(fields):
    return pl.pallas_call(
        rows_kernel,
        out_shape=jax.ShapeDtypeStruct((fields.shape[0] * X * HALF, 2 * Z), bf16),
        in_specs=[VMEM],
        out_specs=VMEM,
        cost_estimate=pl.CostEstimate(flops=0, bytes_accessed=10**6, transcendentals=0),
        compiler_params=GRANT,
        name="as_rows",
    )(fields)


COST = pl.CostEstimate(flops=4 * 10**9, bytes_accessed=3 * 10**6, transcendentals=0)
WORK = pltpu.VMEM((X, Y, 4 * Z), f32)


def own_call(trial, partner, other, tabs):
    return pl.pallas_call(
        own_kernel,
        out_shape=(
            jax.ShapeDtypeStruct((X, HALF, 2 * Z), f32),
            jax.ShapeDtypeStruct((X * Y, 4 * Z), bf16),
        ),
        in_specs=[VMEM] * 5,
        out_specs=(VMEM, VMEM),
        scratch_shapes=[WORK],
        cost_estimate=COST,
        compiler_params=GRANT,
        name="own_terms",
    )(trial, partner, other, *tabs)


def cross_call(trial, pairs, own, tabs):
    return pl.pallas_call(
        cross_kernel,
        out_shape=jax.ShapeDtypeStruct((X, Y, 2 * Z), bf16),
        in_specs=[VMEM] * 5,
        out_specs=VMEM,
        scratch_shapes=[WORK],
        cost_estimate=COST,
        compiler_params=GRANT,
        name="cross_terms",
    )(trial, pairs, own, *tabs)


LOW = 4


def trial_route(blocks, groups):
    half = blocks // 2
    pairs = []
    for block in range(blocks):
        source = (block + 2) % blocks
        for group in range(groups):
            place = group % LOW
            if source // half != block // half:
                if block % 2 == 0:
                    place = LOW - 1 - place
                else:
                    place = (place + (1 if block >= half else LOW - 1)) % LOW
            pairs.append((source * groups + group // LOW * LOW + place, block * groups + group))
    return pairs


def slab_route(blocks, groups):
    half = blocks // 2
    pairs = []
    for block in range(blocks):
        owner = (block + 2) % blocks
        for group in range(groups):
            mirror = group // LOW * LOW + LOW - 1 - group % LOW
            place = mirror if owner // half != block // half else group
            pairs.append((block * groups + group, owner * groups + place))
    return pairs


def local(targets, partners):
    blocks, groups = lax.axis_size("orb"), lax.axis_size("grp")
    tabs = tables()
    target = as_rows(targets)
    remote = lax.ppermute(target, ("orb", "grp"), trial_route(blocks, groups))
    partner = as_rows(partners)
    other = lax.ppermute(partner, "orb", [(i ^ 1, i) for i in range(blocks)])
    own, pairs = own_call(target, partner, other, tabs)
    fields = cross_call(remote, pairs, own, tabs)
    slabs = lax.all_to_all(fields, "grp", 0, 0, tiled=True)
    summed = jnp.sum(slabs.astype(f32), axis=0)
    ahead = lax.ppermute(summed[HALF:], ("orb", "grp"), slab_route(blocks, groups))
    factor = -1.0 / math.sqrt(STEPS * groups * 2)
    return ((summed[:HALF] + ahead) * factor).reshape(1, Y * Z)


def solution(mesh):
    in_specs = (P("orb", None), P(("orb", "grp"), None))
    out_specs = P("orb", "grp")
    return jax.shard_map(local, mesh=mesh, in_specs=in_specs, out_specs=out_specs, check_vma=False)
```

```python
import math

import jax
import jax.numpy as jnp
import numpy as np
from jax import lax
from jax.experimental import pallas as pl
from jax.experimental.pallas import tpu as pltpu
from jax.sharding import PartitionSpec as P

X = 32
Y = 48
Z = 64
HALF = Y // 2
STEPS = 3
XB = 4
ROWS = XB * Y
GROUPS = X // XB
SIDE = 256

screening = 0.11
spacing = 0.45

bf16 = jnp.bfloat16
f32 = jnp.float32


def hartley(length):
    indices = np.arange(length)
    angles = 2.0 * np.pi / length * (indices[:, None] * indices[None, :] % length)
    return (np.cos(angles) + np.sin(angles)).astype(np.float32)


def squared_wave(length):
    indices = np.arange(length)
    folded = np.minimum(indices, length - indices)
    return (2.0 * np.pi / (length * spacing) * folded) ** 2


def coulomb_table():
    squares = (
        squared_wave(X)[:, None, None]
        + squared_wave(Y)[None, :, None]
        + squared_wave(Z)[None, None, :]
    )
    positive = squares > 0.0
    guarded = np.where(positive, squares, 1.0)
    screened = 4.0 * np.pi * (1.0 - np.exp(-guarded / (4.0 * screening * screening))) / guarded
    kernel = np.where(positive, screened, np.pi / (screening * screening))
    spread = np.sqrt(np.mean(kernel * kernel))
    return (kernel / (spread * (X * Y * Z))).astype(np.float32)


def tables():
    order = 2 * (np.arange(Y) % HALF) + np.arange(Y) // HALF
    along_y = hartley(Y)[:, order]
    joined = np.zeros((SIDE, 4 * SIDE), np.float32)
    joined[:, :SIDE] = np.kron(np.eye(4, dtype=np.float32), hartley(Z))
    joined[:, SIDE : 2 * SIDE] = np.kron(hartley(X), np.eye(8, dtype=np.float32))
    joined[:ROWS, 2 * SIDE : 2 * SIDE + ROWS] = np.kron(np.eye(XB, dtype=np.float32), along_y)
    joined[:ROWS, 3 * SIDE : 3 * SIDE + ROWS] = np.kron(np.eye(XB, dtype=np.float32), along_y.T)
    kernel = jnp.asarray(np.tile(coulomb_table(), (1, 1, 2)))
    return jnp.asarray(joined.astype(bf16)), kernel


def views(joined):
    return (
        joined.at[:, :SIDE],
        joined.at[:, SIDE : 2 * SIDE],
        joined.at[:ROWS, 2 * SIDE : 2 * SIDE + ROWS],
        joined.at[:ROWS, 3 * SIDE : 3 * SIDE + ROWS],
    )


def low_half(shape):
    return lax.broadcasted_iota(jnp.int32, shape, len(shape) - 1) < Z


def spread_rows(first, second):
    first = first.astype(f32).reshape(XB, HALF, 2 * Z)
    second = second.astype(f32).reshape(XB, HALF, 2 * Z)
    low = low_half(first.shape)
    even = jnp.where(low, first, pltpu.roll(second, Z, 2))
    odd = jnp.where(low, pltpu.roll(first, Z, 2), second)
    return jnp.concatenate([even, odd], axis=1).reshape(ROWS, 2 * Z).astype(bf16)


def gather_rows(field):
    planes = field.reshape(XB, Y, 2 * Z)
    planes = planes + pltpu.roll(planes, Z, 2)
    even, odd = planes[:, :HALF], planes[:, HALF:]
    return jnp.where(low_half(even.shape), even, odd)


def dot(a, b):
    return jnp.dot(a, b, preferred_element_type=f32)


def middle(work, x8, kernel, lanes):
    for block in range(Y // 8):
        rows = slice(block * 8, block * 8 + 8)
        field = work[:, rows, :].reshape(X * 8, lanes).astype(bf16)
        scale = kernel[:, rows, :].reshape(X * 8, 2 * Z)
        scale = jnp.concatenate([scale] * (lanes // (2 * Z)), axis=1)
        field = dot(x8[...], field)
        field = dot(x8[...], (field * scale).astype(bf16))
        work[:, rows, :] = field.reshape(X, 8, lanes)


def chunk(step, high, base=0):
    return pl.ds(pl.multiple_of(step * high + base, high), high)


def density(trial, partner):
    trial = spread_rows(trial, trial)
    return jnp.concatenate([trial * partner[:, : 2 * Z], trial * partner[:, 2 * Z :]], axis=1)


def inward(field, z4, y_in):
    return dot(y_in[...], dot(field, z4[...]).astype(bf16)).reshape(XB, Y, 4 * Z)


def outward(work, step, partner, both, z4, y_out):
    field = work[pl.ds(step * XB, XB)].reshape(ROWS, 4 * Z).astype(bf16)
    field = dot(dot(y_out[...], field).astype(bf16), z4[...]) * partner.astype(f32)
    return gather_rows(field[:, : 2 * Z] + jnp.where(both, field[:, 2 * Z :], 0.0))


def own_kernel(t_ref, p_ref, q_ref, joined, kernel, o_ref, pairs, work):
    z4, x8, y_in, y_out = views(joined)
    odd = lax.axis_index("orb") % 2 == 1
    high = XB * HALF
    for step in range(GROUPS):
        rows, rows2 = chunk(step, high), chunk(step, high, X * HALF)
        partner = jnp.concatenate(
            [
                spread_rows(p_ref[rows, :], p_ref[rows2, :]),
                spread_rows(q_ref[rows, :], q_ref[rows2, :]),
            ],
            axis=1,
        )
        pairs[chunk(step, ROWS), :] = partner
        work[pl.ds(step * XB, XB)] = inward(density(t_ref[rows, :], partner), z4, y_in)
    middle(work, x8, kernel, 4 * Z)
    for step in range(GROUPS):
        partner = pairs[chunk(step, ROWS), :]
        o_ref[pl.ds(step * XB, XB)] = outward(work, step, partner, odd, z4, y_out)


def cross_kernel(r_ref, t_ref, c_ref, pairs, own_ref, joined, kernel, o_ref, work, first):
    z4, x8, y_in, y_out = views(joined)
    block = lax.axis_index("orb")
    half = lax.axis_size("orb") // 2
    even = block % 2 == 0
    border = block % half >= half - 2
    high = XB * HALF
    for step in range(GROUPS):
        rows, rows2 = chunk(step, high), chunk(step, high, X * HALF)
        trial = jnp.where(even, r_ref[rows, :].astype(f32), t_ref[rows, :].astype(f32))
        kept = pairs[chunk(step, ROWS), :]
        carried = spread_rows(c_ref[rows, :], c_ref[rows2, :])
        partner = jnp.where(even, kept[:, : 2 * Z].astype(f32), carried.astype(f32)).astype(bf16)
        first[chunk(step, ROWS), :] = partner
        partner = jnp.concatenate([partner, kept[:, 2 * Z :]], axis=1)
        work[pl.ds(step * XB, XB)] = inward(density(trial, partner), z4, y_in)
    middle(work, x8, kernel, 4 * Z)
    for step in range(GROUPS):
        rows = chunk(step, ROWS)
        partner = jnp.concatenate([first[rows, :], pairs[rows, 2 * Z :]], axis=1)
        cross = outward(work, step, partner, even, z4, y_out)
        planes = pl.ds(step * XB, XB)
        own = own_ref[planes] + jnp.where(even, 0.0, cross)
        turned = jnp.concatenate([cross[i : i + 1] for i in reversed(range(XB))], axis=0)
        cross = jnp.where(border, turned, cross)
        o_ref[planes] = jnp.concatenate([own, cross], axis=1).astype(bf16)


def rows_kernel(x_ref, o_ref):
    o_ref[...] = x_ref[...].reshape(o_ref.shape)


VMEM = pl.BlockSpec(memory_space=pltpu.VMEM)
GRANT = pltpu.CompilerParams(vmem_limit_bytes=16 * 2**20)


def as_rows(fields):
    return pl.pallas_call(
        rows_kernel,
        out_shape=jax.ShapeDtypeStruct((fields.shape[0] * X * HALF, 2 * Z), bf16),
        in_specs=[VMEM],
        out_specs=VMEM,
        cost_estimate=pl.CostEstimate(flops=0, bytes_accessed=10**6, transcendentals=0),
        compiler_params=GRANT,
        name="as_rows",
    )(fields)


COST = pl.CostEstimate(flops=4 * 10**9, bytes_accessed=3 * 10**6, transcendentals=0)
WORK = pltpu.VMEM((X, Y, 4 * Z), f32)


def own_call(trial, partner, other, tabs):
    return pl.pallas_call(
        own_kernel,
        out_shape=(
            jax.ShapeDtypeStruct((X, HALF, 2 * Z), f32),
            jax.ShapeDtypeStruct((X * Y, 4 * Z), bf16),
        ),
        in_specs=[VMEM] * 5,
        out_specs=(VMEM, VMEM),
        scratch_shapes=[WORK],
        cost_estimate=COST,
        compiler_params=GRANT,
        name="own_terms",
    )(trial, partner, other, *tabs)


def cross_call(remote, trial, carried, pairs, own, tabs):
    return pl.pallas_call(
        cross_kernel,
        out_shape=jax.ShapeDtypeStruct((X, Y, 2 * Z), bf16),
        in_specs=[VMEM] * 7,
        out_specs=VMEM,
        scratch_shapes=[WORK, pltpu.VMEM((X * Y, 2 * Z), bf16)],
        cost_estimate=COST,
        compiler_params=GRANT,
        name="cross_terms",
    )(remote, trial, carried, pairs, own, *tabs)


LOW = 4


def route(blocks, groups, distance, parity):
    half = blocks // 2
    pairs = []
    for block in range(parity, blocks, 2):
        target = (block + distance) % blocks
        for group in range(groups):
            mirror = group // LOW * LOW + LOW - 1 - group % LOW
            place = mirror if target // half != block // half else group
            pairs.append((block * groups + group, target * groups + place))
    return pairs


def local(targets, partners):
    blocks, groups = lax.axis_size("orb"), lax.axis_size("grp")
    send = lambda what, distance, parity: lax.ppermute(
        what, ("orb", "grp"), route(blocks, groups, distance, parity)
    )
    tabs = tables()
    target = as_rows(targets)
    remote = send(target, -2, 0)
    partner = as_rows(partners)
    carried = send(partner, 2, 1)
    other = lax.ppermute(partner, "orb", [(i ^ 1, i) for i in range(blocks)])
    own, pairs = own_call(target, partner, other, tabs)
    fields = cross_call(remote, target, carried, pairs, own, tabs)
    slabs = lax.all_to_all(fields, "grp", 0, 0, tiled=True)
    summed = jnp.sum(slabs.astype(f32), axis=0)
    ahead = send(summed[HALF:], 2, 0)
    factor = -1.0 / math.sqrt(STEPS * groups * 2)
    return ((summed[:HALF] + ahead) * factor).reshape(1, Y * Z)


def solution(mesh):
    in_specs = (P("orb", None), P(("orb", "grp"), None))
    out_specs = P("orb", "grp")
    return jax.shard_map(local, mesh=mesh, in_specs=in_specs, out_specs=out_specs, check_vma=False)
```

```python
import math

import jax
import jax.numpy as jnp
import numpy as np
from jax import lax
from jax.experimental import pallas as pl
from jax.experimental.pallas import tpu as pltpu
from jax.sharding import PartitionSpec as P

X = 32
Y = 48
Z = 64
HALF = Y // 2
STEPS = 3
XB = 4
ROWS = XB * Y
GROUPS = X // XB
SIDE = 256

screening = 0.11
spacing = 0.45

bf16 = jnp.bfloat16
f32 = jnp.float32


def hartley(length):
    indices = np.arange(length)
    angles = 2.0 * np.pi / length * (indices[:, None] * indices[None, :] % length)
    return (np.cos(angles) + np.sin(angles)).astype(np.float32)


def squared_wave(length):
    indices = np.arange(length)
    folded = np.minimum(indices, length - indices)
    return (2.0 * np.pi / (length * spacing) * folded) ** 2


def coulomb_table():
    squares = (
        squared_wave(X)[:, None, None]
        + squared_wave(Y)[None, :, None]
        + squared_wave(Z)[None, None, :]
    )
    positive = squares > 0.0
    guarded = np.where(positive, squares, 1.0)
    screened = 4.0 * np.pi * (1.0 - np.exp(-guarded / (4.0 * screening * screening))) / guarded
    kernel = np.where(positive, screened, np.pi / (screening * screening))
    spread = np.sqrt(np.mean(kernel * kernel))
    return (kernel / (spread * (X * Y * Z))).astype(np.float32)


def tables():
    order = 2 * (np.arange(Y) % HALF) + np.arange(Y) // HALF
    along_y = hartley(Y)[:, order]
    joined = np.zeros((SIDE, 4 * SIDE), np.float32)
    joined[:, :SIDE] = np.kron(np.eye(4, dtype=np.float32), hartley(Z))
    joined[:, SIDE : 2 * SIDE] = np.kron(hartley(X), np.eye(8, dtype=np.float32))
    joined[:ROWS, 2 * SIDE : 2 * SIDE + ROWS] = np.kron(np.eye(XB, dtype=np.float32), along_y)
    joined[:ROWS, 3 * SIDE : 3 * SIDE + ROWS] = np.kron(np.eye(XB, dtype=np.float32), along_y.T)
    kernel = jnp.asarray(np.tile(coulomb_table(), (1, 1, 2)))
    return jnp.asarray(joined.astype(bf16)), kernel


def views(joined):
    return (
        joined.at[:, :SIDE],
        joined.at[:, SIDE : 2 * SIDE],
        joined.at[:ROWS, 2 * SIDE : 2 * SIDE + ROWS],
        joined.at[:ROWS, 3 * SIDE : 3 * SIDE + ROWS],
    )


def low_half(shape):
    return lax.broadcasted_iota(jnp.int32, shape, len(shape) - 1) < Z


def spread_rows(first, second):
    first = first.astype(f32).reshape(XB, HALF, 2 * Z)
    second = second.astype(f32).reshape(XB, HALF, 2 * Z)
    low = low_half(first.shape)
    even = jnp.where(low, first, pltpu.roll(second, Z, 2))
    odd = jnp.where(low, pltpu.roll(first, Z, 2), second)
    return jnp.concatenate([even, odd], axis=1).reshape(ROWS, 2 * Z).astype(bf16)


def gather_rows(field):
    planes = field.reshape(XB, Y, 2 * Z)
    planes = planes + pltpu.roll(planes, Z, 2)
    even, odd = planes[:, :HALF], planes[:, HALF:]
    return jnp.where(low_half(even.shape), even, odd)


def dot(a, b):
    return jnp.dot(a, b, preferred_element_type=f32)


def middle(work, x8, kernel, lanes):
    for block in range(Y // 8):
        rows = slice(block * 8, block * 8 + 8)
        field = work[:, rows, :].reshape(X * 8, lanes).astype(bf16)
        scale = kernel[:, rows, :].reshape(X * 8, 2 * Z)
        scale = jnp.concatenate([scale] * (lanes // (2 * Z)), axis=1)
        field = dot(x8[...], field)
        field = dot(x8[...], (field * scale).astype(bf16))
        work[:, rows, :] = field.reshape(X, 8, lanes)


def chunk(step, high, base=0):
    return pl.ds(pl.multiple_of(step * high + base, high), high)


def inward(trial, partner, z, y_in):
    trial = spread_rows(trial, trial)
    parts = [trial * partner[:, at : at + 2 * Z] for at in range(0, partner.shape[1], 2 * Z)]
    field = dot(jnp.concatenate(parts, axis=1), z).astype(bf16)
    return dot(y_in[...], field).reshape(XB, Y, partner.shape[1])


def outward(field, partner, z, y_out):
    field = field.reshape(ROWS, partner.shape[1]).astype(bf16)
    field = dot(dot(y_out[...], field).astype(bf16), z) * partner.astype(f32)
    return gather_rows(sum(field[:, at : at + 2 * Z] for at in range(0, field.shape[1], 2 * Z)))


def own_kernel(t_ref, p_ref, joined, kernel, o_ref, mine, work):
    z4, x8, y_in, y_out = views(joined)
    z = z4[: 2 * Z, : 2 * Z]
    high = XB * HALF
    for step in range(GROUPS):
        rows, rows2 = chunk(step, high), chunk(step, high, X * HALF)
        partner = spread_rows(p_ref[rows, :], p_ref[rows2, :])
        mine[chunk(step, ROWS), :] = partner
        work[pl.ds(step * XB, XB)] = inward(t_ref[rows, :], partner, z, y_in)
    middle(work, x8, kernel, 2 * Z)
    for step in range(GROUPS):
        planes = pl.ds(step * XB, XB)
        o_ref[planes] = outward(work[planes], mine[chunk(step, ROWS), :], z, y_out)


def cross_kernel(r_ref, t_ref, c_ref, q_ref, mine, own_ref, joined, kernel, o_ref, work, pairs):
    z4, x8, y_in, y_out = views(joined)
    block = lax.axis_index("orb")
    half = lax.axis_size("orb") // 2
    even = block % 2 == 0
    border = block % half >= half - 2
    high = XB * HALF
    for step in range(GROUPS):
        rows, rows2 = chunk(step, high), chunk(step, high, X * HALF)
        trial = jnp.where(even, r_ref[rows, :].astype(f32), t_ref[rows, :].astype(f32))
        carried = spread_rows(c_ref[rows, :], c_ref[rows2, :]).astype(f32)
        first = jnp.where(even, mine[chunk(step, ROWS), :].astype(f32), carried).astype(bf16)
        second = spread_rows(q_ref[rows, :], q_ref[rows2, :])
        partner = jnp.concatenate([first, second], axis=1)
        pairs[chunk(step, ROWS), :] = partner
        work[pl.ds(step * XB, XB)] = inward(trial, partner, z4[...], y_in)
    middle(work, x8, kernel, 4 * Z)
    for step in range(GROUPS):
        planes = pl.ds(step * XB, XB)
        cross = outward(work[planes], pairs[chunk(step, ROWS), :], z4[...], y_out)
        own = own_ref[planes] + jnp.where(even, 0.0, cross)
        turned = jnp.concatenate([cross[i : i + 1] for i in reversed(range(XB))], axis=0)
        cross = jnp.where(border, turned, cross)
        o_ref[planes] = jnp.concatenate([own, cross], axis=1).astype(bf16)


def rows_kernel(x_ref, o_ref):
    o_ref[...] = x_ref[...].reshape(o_ref.shape)


VMEM = pl.BlockSpec(memory_space=pltpu.VMEM)
GRANT = pltpu.CompilerParams(vmem_limit_bytes=16 * 2**20)


def as_rows(fields):
    return pl.pallas_call(
        rows_kernel,
        out_shape=jax.ShapeDtypeStruct((fields.shape[0] * X * HALF, 2 * Z), bf16),
        in_specs=[VMEM],
        out_specs=VMEM,
        cost_estimate=pl.CostEstimate(flops=0, bytes_accessed=10**6, transcendentals=0),
        compiler_params=GRANT,
        name="as_rows",
    )(fields)


COST = pl.CostEstimate(flops=4 * 10**9, bytes_accessed=3 * 10**6, transcendentals=0)


def own_call(trial, partner, tabs):
    return pl.pallas_call(
        own_kernel,
        out_shape=(
            jax.ShapeDtypeStruct((X, HALF, 2 * Z), f32),
            jax.ShapeDtypeStruct((X * Y, 2 * Z), bf16),
        ),
        in_specs=[VMEM] * 4,
        out_specs=(VMEM, VMEM),
        scratch_shapes=[pltpu.VMEM((X, Y, 2 * Z), f32)],
        cost_estimate=COST,
        compiler_params=GRANT,
        name="own_terms",
    )(trial, partner, *tabs)


def cross_call(remote, trial, carried, other, mine, own, tabs):
    return pl.pallas_call(
        cross_kernel,
        out_shape=jax.ShapeDtypeStruct((X, Y, 2 * Z), bf16),
        in_specs=[VMEM] * 8,
        out_specs=VMEM,
        scratch_shapes=[pltpu.VMEM((X, Y, 4 * Z), f32), pltpu.VMEM((X * Y, 4 * Z), bf16)],
        cost_estimate=COST,
        compiler_params=GRANT,
        name="cross_terms",
    )(remote, trial, carried, other, mine, own, *tabs)


LOW = 4


def route(blocks, groups, distance, parity):
    half = blocks // 2
    pairs = []
    for block in range(parity, blocks, 2):
        target = (block + distance) % blocks
        for group in range(groups):
            mirror = group // LOW * LOW + LOW - 1 - group % LOW
            place = mirror if target // half != block // half else group
            pairs.append((block * groups + group, target * groups + place))
    return pairs


def local(targets, partners):
    blocks, groups = lax.axis_size("orb"), lax.axis_size("grp")
    send = lambda what, distance, parity: lax.ppermute(
        what, ("orb", "grp"), route(blocks, groups, distance, parity)
    )
    tabs = tables()
    target = as_rows(targets)
    remote = send(target, -2, 0)
    partner = as_rows(partners)
    carried = send(partner, 2, 1)
    other = lax.ppermute(partner, "orb", [(i ^ 1, i) for i in range(blocks)])
    own, mine = own_call(target, partner, tabs)
    fields = cross_call(remote, target, carried, other, mine, own, tabs)
    slabs = lax.all_to_all(fields, "grp", 0, 0, tiled=True)
    summed = jnp.sum(slabs.astype(f32), axis=0)
    ahead = send(summed[HALF:], 2, 0)
    factor = -1.0 / math.sqrt(STEPS * groups * 2)
    return ((summed[:HALF] + ahead) * factor).reshape(1, Y * Z)


def solution(mesh):
    in_specs = (P("orb", None), P(("orb", "grp"), None))
    out_specs = P("orb", "grp")
    return jax.shard_map(local, mesh=mesh, in_specs=in_specs, out_specs=out_specs, check_vma=False)
```

```python
import math

import jax
import jax.numpy as jnp
import numpy as np
from jax import lax
from jax.experimental import pallas as pl
from jax.experimental.pallas import tpu as pltpu
from jax.sharding import PartitionSpec as P

X = 32
Y = 48
Z = 64
HALF = Y // 2
STEPS = 3
XB = 4
ROWS = XB * Y
GROUPS = X // XB
SIDE = 256

screening = 0.11
spacing = 0.45

bf16 = jnp.bfloat16
f32 = jnp.float32


def hartley(length):
    indices = np.arange(length)
    angles = 2.0 * np.pi / length * (indices[:, None] * indices[None, :] % length)
    return (np.cos(angles) + np.sin(angles)).astype(np.float32)


def squared_wave(length):
    indices = np.arange(length)
    folded = np.minimum(indices, length - indices)
    return (2.0 * np.pi / (length * spacing) * folded) ** 2


def coulomb_table():
    squares = (
        squared_wave(X)[:, None, None]
        + squared_wave(Y)[None, :, None]
        + squared_wave(Z)[None, None, :]
    )
    positive = squares > 0.0
    guarded = np.where(positive, squares, 1.0)
    screened = 4.0 * np.pi * (1.0 - np.exp(-guarded / (4.0 * screening * screening))) / guarded
    kernel = np.where(positive, screened, np.pi / (screening * screening))
    spread = np.sqrt(np.mean(kernel * kernel))
    return (kernel / (spread * (X * Y * Z))).astype(np.float32)


def tables():
    order = 2 * (np.arange(Y) % HALF) + np.arange(Y) // HALF
    along_y = hartley(Y)[:, order]
    joined = np.zeros((SIDE, 4 * SIDE), np.float32)
    joined[:, :SIDE] = np.kron(np.eye(4, dtype=np.float32), hartley(Z))
    joined[:, SIDE : 2 * SIDE] = np.kron(hartley(X), np.eye(8, dtype=np.float32))
    joined[:ROWS, 2 * SIDE : 2 * SIDE + ROWS] = np.kron(np.eye(XB, dtype=np.float32), along_y)
    joined[:ROWS, 3 * SIDE : 3 * SIDE + ROWS] = np.kron(np.eye(XB, dtype=np.float32), along_y.T)
    kernel = jnp.asarray(np.tile(coulomb_table(), (1, 1, 2)))
    return jnp.asarray(joined.astype(bf16)), kernel


def views(joined):
    return (
        joined.at[:, :SIDE],
        joined.at[:, SIDE : 2 * SIDE],
        joined.at[:ROWS, 2 * SIDE : 2 * SIDE + ROWS],
        joined.at[:ROWS, 3 * SIDE : 3 * SIDE + ROWS],
    )


def low_half(shape):
    return lax.broadcasted_iota(jnp.int32, shape, len(shape) - 1) < Z


def spread_rows(first, second):
    first = first.astype(f32).reshape(XB, HALF, 2 * Z)
    second = second.astype(f32).reshape(XB, HALF, 2 * Z)
    low = low_half(first.shape)
    even = jnp.where(low, first, pltpu.roll(second, Z, 2))
    odd = jnp.where(low, pltpu.roll(first, Z, 2), second)
    return jnp.concatenate([even, odd], axis=1).reshape(ROWS, 2 * Z).astype(bf16)


def gather_rows(field):
    planes = field.reshape(XB, Y, 2 * Z)
    planes = planes + pltpu.roll(planes, Z, 2)
    even, odd = planes[:, :HALF], planes[:, HALF:]
    return jnp.where(low_half(even.shape), even, odd)


def dot(a, b):
    return jnp.dot(a, b, preferred_element_type=f32)


def middle(work, x8, kernel, lanes):
    together = 4 * Z // lanes
    for block in range(0, Y // 8, together):
        groups = [slice(at * 8, at * 8 + 8) for at in range(block, block + together)]
        field = jnp.concatenate([work[:, g, :].reshape(X * 8, lanes) for g in groups], axis=1)
        scale = [kernel[:, g, :].reshape(X * 8, 2 * Z) for g in groups]
        scale = jnp.concatenate([t for t in scale for _ in range(lanes // (2 * Z))], axis=1)
        field = dot(x8[...], field.astype(bf16))
        field = dot(x8[...], (field * scale).astype(bf16))
        for at, g in enumerate(groups):
            work[:, g, :] = field[:, at * lanes : (at + 1) * lanes].reshape(X, 8, lanes)


def chunk(step, high, base=0):
    return pl.ds(pl.multiple_of(step * high + base, high), high)


def inward(trial, partner, z, y_in):
    trial = spread_rows(trial, trial)
    parts = [trial * partner[:, at : at + 2 * Z] for at in range(0, partner.shape[1], 2 * Z)]
    field = dot(jnp.concatenate(parts, axis=1), z).astype(bf16)
    return dot(y_in[...], field).reshape(XB, Y, partner.shape[1])


def outward(field, partner, z, y_out):
    field = field.reshape(ROWS, partner.shape[1]).astype(bf16)
    field = dot(dot(y_out[...], field).astype(bf16), z) * partner.astype(f32)
    return gather_rows(sum(field[:, at : at + 2 * Z] for at in range(0, field.shape[1], 2 * Z)))


def own_kernel(t_ref, p_ref, joined, kernel, o_ref, mine, work):
    z4, x8, y_in, y_out = views(joined)
    high = XB * HALF
    halves = [slice(0, 2 * Z), slice(2 * Z, 4 * Z)]
    for step in range(0, GROUPS, 2):
        density = []
        for at in (step, step + 1):
            rows, rows2 = chunk(at, high), chunk(at, high, X * HALF)
            partner = spread_rows(p_ref[rows, :], p_ref[rows2, :])
            mine[chunk(at, ROWS), :] = partner
            density.append(spread_rows(t_ref[rows, :], t_ref[rows, :]) * partner)
        field = dot(jnp.concatenate(density, axis=1), z4[...]).astype(bf16)
        field = dot(y_in[...], field)
        for at, lanes in zip((step, step + 1), halves):
            work[pl.ds(at * XB, XB)] = field[:, lanes].reshape(XB, Y, 2 * Z)
    middle(work, x8, kernel, 2 * Z)
    for step in range(0, GROUPS, 2):
        field = [work[pl.ds(at * XB, XB)].reshape(ROWS, 2 * Z) for at in (step, step + 1)]
        field = jnp.concatenate(field, axis=1).astype(bf16)
        field = dot(dot(y_out[...], field).astype(bf16), z4[...])
        for at, lanes in zip((step, step + 1), halves):
            partner = mine[chunk(at, ROWS), :].astype(f32)
            o_ref[pl.ds(at * XB, XB)] = gather_rows(field[:, lanes] * partner)


def cross_kernel(r_ref, t_ref, c_ref, q_ref, mine, own_ref, joined, kernel, o_ref, work, pairs):
    z4, x8, y_in, y_out = views(joined)
    block = lax.axis_index("orb")
    half = lax.axis_size("orb") // 2
    even = block % 2 == 0
    border = block % half >= half - 2
    high = XB * HALF
    for step in range(GROUPS):
        rows, rows2 = chunk(step, high), chunk(step, high, X * HALF)
        trial = jnp.where(even, r_ref[rows, :].astype(f32), t_ref[rows, :].astype(f32))
        carried = spread_rows(c_ref[rows, :], c_ref[rows2, :]).astype(f32)
        first = jnp.where(even, mine[chunk(step, ROWS), :].astype(f32), carried).astype(bf16)
        second = spread_rows(q_ref[rows, :], q_ref[rows2, :])
        partner = jnp.concatenate([first, second], axis=1)
        pairs[chunk(step, ROWS), :] = partner
        work[pl.ds(step * XB, XB)] = inward(trial, partner, z4[...], y_in)
    middle(work, x8, kernel, 4 * Z)
    for step in range(GROUPS):
        planes = pl.ds(step * XB, XB)
        cross = outward(work[planes], pairs[chunk(step, ROWS), :], z4[...], y_out)
        own = own_ref[planes] + jnp.where(even, 0.0, cross)
        turned = jnp.concatenate([cross[i : i + 1] for i in reversed(range(XB))], axis=0)
        cross = jnp.where(border, turned, cross)
        o_ref[planes] = jnp.concatenate([own, cross], axis=1).astype(bf16)


def rows_kernel(x_ref, o_ref):
    o_ref[...] = x_ref[...].reshape(o_ref.shape)


VMEM = pl.BlockSpec(memory_space=pltpu.VMEM)
GRANT = pltpu.CompilerParams(vmem_limit_bytes=16 * 2**20)


def as_rows(fields):
    return pl.pallas_call(
        rows_kernel,
        out_shape=jax.ShapeDtypeStruct((fields.shape[0] * X * HALF, 2 * Z), bf16),
        in_specs=[VMEM],
        out_specs=VMEM,
        cost_estimate=pl.CostEstimate(flops=0, bytes_accessed=10**6, transcendentals=0),
        compiler_params=GRANT,
        name="as_rows",
    )(fields)


COST = pl.CostEstimate(flops=4 * 10**9, bytes_accessed=3 * 10**6, transcendentals=0)


def own_call(trial, partner, tabs):
    return pl.pallas_call(
        own_kernel,
        out_shape=(
            jax.ShapeDtypeStruct((X, HALF, 2 * Z), f32),
            jax.ShapeDtypeStruct((X * Y, 2 * Z), bf16),
        ),
        in_specs=[VMEM] * 4,
        out_specs=(VMEM, VMEM),
        scratch_shapes=[pltpu.VMEM((X, Y, 2 * Z), f32)],
        cost_estimate=COST,
        compiler_params=GRANT,
        name="own_terms",
    )(trial, partner, *tabs)


def cross_call(remote, trial, carried, other, mine, own, tabs):
    return pl.pallas_call(
        cross_kernel,
        out_shape=jax.ShapeDtypeStruct((X, Y, 2 * Z), bf16),
        in_specs=[VMEM] * 8,
        out_specs=VMEM,
        scratch_shapes=[pltpu.VMEM((X, Y, 4 * Z), f32), pltpu.VMEM((X * Y, 4 * Z), bf16)],
        cost_estimate=COST,
        compiler_params=GRANT,
        name="cross_terms",
    )(remote, trial, carried, other, mine, own, *tabs)


LOW = 4


def route(blocks, groups, distance, parity):
    half = blocks // 2
    pairs = []
    for block in range(parity, blocks, 2):
        target = (block + distance) % blocks
        for group in range(groups):
            mirror = group // LOW * LOW + LOW - 1 - group % LOW
            place = mirror if target // half != block // half else group
            pairs.append((block * groups + group, target * groups + place))
    return pairs


def local(targets, partners):
    blocks, groups = lax.axis_size("orb"), lax.axis_size("grp")
    send = lambda what, distance, parity: lax.ppermute(
        what, ("orb", "grp"), route(blocks, groups, distance, parity)
    )
    tabs = tables()
    target = as_rows(targets)
    remote = send(target, -2, 0)
    partner = as_rows(partners)
    carried = send(partner, 2, 1)
    other = lax.ppermute(partner, "orb", [(i ^ 1, i) for i in range(blocks)])
    own, mine = own_call(target, partner, tabs)
    fields = cross_call(remote, target, carried, other, mine, own, tabs)
    slabs = lax.all_to_all(fields, "grp", 0, 0, tiled=True)
    summed = jnp.sum(slabs.astype(f32), axis=0)
    ahead = send(summed[HALF:], 2, 0)
    factor = -1.0 / math.sqrt(STEPS * groups * 2)
    return ((summed[:HALF] + ahead) * factor).reshape(1, Y * Z)


def solution(mesh):
    in_specs = (P("orb", None), P(("orb", "grp"), None))
    out_specs = P("orb", "grp")
    return jax.shard_map(local, mesh=mesh, in_specs=in_specs, out_specs=out_specs, check_vma=False)
```

```python
import math

import jax
import jax.numpy as jnp
import numpy as np
from jax import lax
from jax.experimental import pallas as pl
from jax.experimental.pallas import tpu as pltpu
from jax.sharding import PartitionSpec as P

X = 32
Y = 48
Z = 64
HALF = Y // 2
STEPS = 3
XB = 4
ROWS = XB * Y
GROUPS = X // XB
SIDE = 256

screening = 0.11
spacing = 0.45

bf16 = jnp.bfloat16
f32 = jnp.float32


def hartley(length):
    indices = np.arange(length)
    angles = 2.0 * np.pi / length * (indices[:, None] * indices[None, :] % length)
    return (np.cos(angles) + np.sin(angles)).astype(np.float32)


def squared_wave(length):
    indices = np.arange(length)
    folded = np.minimum(indices, length - indices)
    return (2.0 * np.pi / (length * spacing) * folded) ** 2


def coulomb_table():
    squares = (
        squared_wave(X)[:, None, None]
        + squared_wave(Y)[None, :, None]
        + squared_wave(Z)[None, None, :]
    )
    positive = squares > 0.0
    guarded = np.where(positive, squares, 1.0)
    screened = 4.0 * np.pi * (1.0 - np.exp(-guarded / (4.0 * screening * screening))) / guarded
    kernel = np.where(positive, screened, np.pi / (screening * screening))
    spread = np.sqrt(np.mean(kernel * kernel))
    return (kernel / (spread * (X * Y * Z))).astype(np.float32)


def tables():
    order = 2 * (np.arange(Y) % HALF) + np.arange(Y) // HALF
    along_y = hartley(Y)[:, order]
    joined = np.zeros((SIDE, 4 * SIDE), np.float32)
    joined[:, :SIDE] = np.kron(np.eye(4, dtype=np.float32), hartley(Z))
    joined[:, SIDE : 2 * SIDE] = np.kron(hartley(X), np.eye(8, dtype=np.float32))
    joined[:ROWS, 2 * SIDE : 2 * SIDE + ROWS] = np.kron(np.eye(XB, dtype=np.float32), along_y)
    joined[:ROWS, 3 * SIDE : 3 * SIDE + ROWS] = np.kron(np.eye(XB, dtype=np.float32), along_y.T)
    kernel = jnp.asarray(np.tile(coulomb_table(), (1, 1, 2)))
    return jnp.asarray(joined.astype(bf16)), kernel


def views(joined):
    return (
        joined.at[:, :SIDE],
        joined.at[:, SIDE : 2 * SIDE],
        joined.at[:ROWS, 2 * SIDE : 2 * SIDE + ROWS],
        joined.at[:ROWS, 3 * SIDE : 3 * SIDE + ROWS],
    )


def low_half(shape):
    return lax.broadcasted_iota(jnp.int32, shape, len(shape) - 1) < Z


def spread_rows(first, second):
    first = first.astype(f32).reshape(XB, HALF, 2 * Z)
    second = second.astype(f32).reshape(XB, HALF, 2 * Z)
    low = low_half(first.shape)
    even = jnp.where(low, first, pltpu.roll(second, Z, 2))
    odd = jnp.where(low, pltpu.roll(first, Z, 2), second)
    return jnp.concatenate([even, odd], axis=1).reshape(ROWS, 2 * Z).astype(bf16)


def gather_rows(field):
    planes = field.reshape(XB, Y, 2 * Z)
    planes = planes + pltpu.roll(planes, Z, 2)
    even, odd = planes[:, :HALF], planes[:, HALF:]
    return jnp.where(low_half(even.shape), even, odd)


def dot(a, b):
    return jnp.dot(a, b, preferred_element_type=f32)


def middle(work, x8, kernel, lanes):
    together = 4 * Z // lanes
    for block in range(0, Y // 8, together):
        groups = [slice(at * 8, at * 8 + 8) for at in range(block, block + together)]
        field = jnp.concatenate([work[:, g, :].reshape(X * 8, lanes) for g in groups], axis=1)
        scale = [kernel[:, g, :].reshape(X * 8, 2 * Z) for g in groups]
        scale = jnp.concatenate([t for t in scale for _ in range(lanes // (2 * Z))], axis=1)
        field = dot(x8[...], field.astype(bf16))
        field = dot(x8[...], (field * scale).astype(bf16))
        for at, g in enumerate(groups):
            work[:, g, :] = field[:, at * lanes : (at + 1) * lanes].reshape(X, 8, lanes)


def chunk(step, high, base=0):
    return pl.ds(pl.multiple_of(step * high + base, high), high)


def inward(trial, partner, z, y_in):
    trial = spread_rows(trial, trial)
    parts = [trial * partner[:, at : at + 2 * Z] for at in range(0, partner.shape[1], 2 * Z)]
    field = dot(jnp.concatenate(parts, axis=1), z).astype(bf16)
    return dot(y_in[...], field).reshape(XB, Y, partner.shape[1])


def outward(field, partner, z, y_out):
    field = field.reshape(ROWS, partner.shape[1]).astype(bf16)
    field = dot(dot(y_out[...], field).astype(bf16), z) * partner.astype(f32)
    return gather_rows(sum(field[:, at : at + 2 * Z] for at in range(0, field.shape[1], 2 * Z)))


def own_kernel(t_ref, p_ref, joined, kernel, o_ref, mine, work):
    z4, x8, y_in, y_out = views(joined)
    high = XB * HALF
    halves = [slice(0, 2 * Z), slice(2 * Z, 4 * Z)]
    for step in range(0, GROUPS, 2):
        density = []
        for at in (step, step + 1):
            rows, rows2 = chunk(at, high), chunk(at, high, X * HALF)
            partner = spread_rows(p_ref[rows, :], p_ref[rows2, :])
            mine[chunk(at, ROWS), :] = partner
            density.append(spread_rows(t_ref[rows, :], t_ref[rows, :]) * partner)
        field = dot(jnp.concatenate(density, axis=1), z4[...]).astype(bf16)
        field = dot(y_in[...], field)
        for at, lanes in zip((step, step + 1), halves):
            work[pl.ds(at * XB, XB)] = field[:, lanes].reshape(XB, Y, 2 * Z)
    middle(work, x8, kernel, 2 * Z)
    for step in range(0, GROUPS, 2):
        field = [work[pl.ds(at * XB, XB)].reshape(ROWS, 2 * Z) for at in (step, step + 1)]
        field = jnp.concatenate(field, axis=1).astype(bf16)
        field = dot(dot(y_out[...], field).astype(bf16), z4[...])
        for at, lanes in zip((step, step + 1), halves):
            partner = mine[chunk(at, ROWS), :].astype(f32)
            o_ref[pl.ds(at * XB, XB)] = gather_rows(field[:, lanes] * partner)


def cross_kernel(r_ref, t_ref, c_ref, q_ref, mine, own_ref, joined, kernel, o_ref, work, pairs):
    z4, x8, y_in, y_out = views(joined)
    block = lax.axis_index("orb")
    half = lax.axis_size("orb") // 2
    even = block % 2 == 0
    border = block % half >= half - 2
    high = XB * HALF
    for step in range(GROUPS):
        rows, rows2 = chunk(step, high), chunk(step, high, X * HALF)
        trial = jnp.where(even, r_ref[rows, :].astype(f32), t_ref[rows, :].astype(f32))
        carried = spread_rows(c_ref[rows, :], c_ref[rows2, :]).astype(f32)
        first = jnp.where(even, mine[chunk(step, ROWS), :].astype(f32), carried).astype(bf16)
        second = spread_rows(q_ref[rows, :], q_ref[rows2, :])
        partner = jnp.concatenate([first, second], axis=1)
        pairs[chunk(step, ROWS), :] = partner
        work[pl.ds(step * XB, XB)] = inward(trial, partner, z4[...], y_in)
    middle(work, x8, kernel, 4 * Z)
    for step in range(GROUPS):
        planes = pl.ds(step * XB, XB)
        cross = outward(work[planes], pairs[chunk(step, ROWS), :], z4[...], y_out)
        own = own_ref[planes] + jnp.where(even, 0.0, cross)
        turned = jnp.concatenate([cross[i : i + 1] for i in reversed(range(XB))], axis=0)
        cross = jnp.where(border, turned, cross)
        o_ref[planes] = jnp.concatenate([own, cross], axis=1).astype(bf16)


def rows_kernel(x_ref, o_ref):
    o_ref[...] = x_ref[...].reshape(o_ref.shape)


VMEM = pl.BlockSpec(memory_space=pltpu.VMEM)
GRANT = pltpu.CompilerParams(vmem_limit_bytes=16 * 2**20)


def as_rows(fields):
    return pl.pallas_call(
        rows_kernel,
        out_shape=jax.ShapeDtypeStruct((fields.shape[0] * X * HALF, 2 * Z), bf16),
        in_specs=[VMEM],
        out_specs=VMEM,
        cost_estimate=pl.CostEstimate(flops=0, bytes_accessed=10**6, transcendentals=0),
        compiler_params=GRANT,
        name="as_rows",
    )(fields)


COST = pl.CostEstimate(flops=4 * 10**9, bytes_accessed=3 * 10**6, transcendentals=0)


def own_call(trial, partner, tabs):
    return pl.pallas_call(
        own_kernel,
        out_shape=(
            jax.ShapeDtypeStruct((X, HALF, 2 * Z), f32),
            jax.ShapeDtypeStruct((X * Y, 2 * Z), bf16),
        ),
        in_specs=[VMEM] * 4,
        out_specs=(VMEM, VMEM),
        scratch_shapes=[pltpu.VMEM((X, Y, 2 * Z), f32)],
        cost_estimate=COST,
        compiler_params=GRANT,
        name="own_terms",
    )(trial, partner, *tabs)


def cross_call(remote, trial, carried, other, mine, own, tabs):
    return pl.pallas_call(
        cross_kernel,
        out_shape=jax.ShapeDtypeStruct((X, Y, 2 * Z), bf16),
        in_specs=[VMEM] * 8,
        out_specs=VMEM,
        scratch_shapes=[pltpu.VMEM((X, Y, 4 * Z), f32), pltpu.VMEM((X * Y, 4 * Z), bf16)],
        cost_estimate=COST,
        compiler_params=GRANT,
        name="cross_terms",
    )(remote, trial, carried, other, mine, own, *tabs)


LOW = 4


def route(blocks, groups, distance, parity, cycle=False):
    half = blocks // 2
    pairs = []
    for block in range(parity, blocks, 2):
        target = (block + distance) % blocks
        for group in range(groups):
            place = group % LOW
            if target // half != block // half:
                place = LOW - 1 - place
                if cycle:
                    place = (group + (1 if block >= half else LOW - 1)) % LOW
            place += group // LOW * LOW
            pairs.append((block * groups + group, target * groups + place))
    return pairs


def local(targets, partners):
    blocks, groups = lax.axis_size("orb"), lax.axis_size("grp")
    send = lambda what, *how: lax.ppermute(what, ("orb", "grp"), route(blocks, groups, *how))
    tabs = tables()
    target = as_rows(targets)
    remote = send(target, -2, 0, True)
    partner = as_rows(partners)
    carried = send(partner, 2, 1)
    other = lax.ppermute(partner, "orb", [(i ^ 1, i) for i in range(blocks)])
    own, mine = own_call(target, partner, tabs)
    fields = cross_call(remote, target, carried, other, mine, own, tabs)
    slabs = lax.all_to_all(fields, "grp", 0, 0, tiled=True)
    summed = jnp.sum(slabs.astype(f32), axis=0)
    ahead = send(summed[HALF:], 2, 0)
    factor = -1.0 / math.sqrt(STEPS * groups * 2)
    return ((summed[:HALF] + ahead) * factor).reshape(1, Y * Z)


def solution(mesh):
    in_specs = (P("orb", None), P(("orb", "grp"), None))
    out_specs = P("orb", "grp")
    return jax.shard_map(local, mesh=mesh, in_specs=in_specs, out_specs=out_specs, check_vma=False)
```

```python
import math

import jax
import jax.numpy as jnp
import numpy as np
from jax import lax
from jax.experimental import pallas as pl
from jax.experimental.pallas import tpu as pltpu
from jax.sharding import PartitionSpec as P

X = 32
Y = 48
Z = 64
HALF = Y // 2
STEPS = 3
XB = 4
ROWS = XB * Y
GROUPS = X // XB
SIDE = 256

screening = 0.11
spacing = 0.45

bf16 = jnp.bfloat16
f32 = jnp.float32


def hartley(length):
    indices = np.arange(length)
    angles = 2.0 * np.pi / length * (indices[:, None] * indices[None, :] % length)
    return (np.cos(angles) + np.sin(angles)).astype(np.float32)


def squared_wave(length):
    indices = np.arange(length)
    folded = np.minimum(indices, length - indices)
    return (2.0 * np.pi / (length * spacing) * folded) ** 2


def coulomb_table():
    squares = (
        squared_wave(X)[:, None, None]
        + squared_wave(Y)[None, :, None]
        + squared_wave(Z)[None, None, :]
    )
    positive = squares > 0.0
    guarded = np.where(positive, squares, 1.0)
    screened = 4.0 * np.pi * (1.0 - np.exp(-guarded / (4.0 * screening * screening))) / guarded
    kernel = np.where(positive, screened, np.pi / (screening * screening))
    spread = np.sqrt(np.mean(kernel * kernel))
    return (kernel / (spread * (X * Y * Z))).astype(np.float32)


def tables():
    order = 2 * (np.arange(Y) % HALF) + np.arange(Y) // HALF
    along_y = hartley(Y)[:, order]
    joined = np.zeros((SIDE, 4 * SIDE), np.float32)
    joined[:, :SIDE] = np.kron(np.eye(4, dtype=np.float32), hartley(Z))
    joined[:, SIDE : 2 * SIDE] = np.kron(hartley(X), np.eye(8, dtype=np.float32))
    joined[:ROWS, 2 * SIDE : 2 * SIDE + ROWS] = np.kron(np.eye(XB, dtype=np.float32), along_y)
    joined[:ROWS, 3 * SIDE : 3 * SIDE + ROWS] = np.kron(np.eye(XB, dtype=np.float32), along_y.T)
    kernel = jnp.asarray(np.tile(coulomb_table(), (1, 1, 2)))
    return jnp.asarray(joined.astype(bf16)), kernel


def views(joined):
    return (
        joined.at[:, :SIDE],
        joined.at[:, SIDE : 2 * SIDE],
        joined.at[:ROWS, 2 * SIDE : 2 * SIDE + ROWS],
        joined.at[:ROWS, 3 * SIDE : 3 * SIDE + ROWS],
    )


def low_half(shape):
    return lax.broadcasted_iota(jnp.int32, shape, len(shape) - 1) < Z


def spread_rows(first, second):
    first = first.astype(f32).reshape(XB, HALF, 2 * Z)
    second = second.astype(f32).reshape(XB, HALF, 2 * Z)
    low = low_half(first.shape)
    even = jnp.where(low, first, pltpu.roll(second, Z, 2))
    odd = jnp.where(low, pltpu.roll(first, Z, 2), second)
    return jnp.concatenate([even, odd], axis=1).reshape(ROWS, 2 * Z).astype(bf16)


def gather_rows(field):
    planes = field.reshape(XB, Y, 2 * Z)
    planes = planes + pltpu.roll(planes, Z, 2)
    even, odd = planes[:, :HALF], planes[:, HALF:]
    return jnp.where(low_half(even.shape), even, odd)


def dot(a, b):
    return jnp.dot(a, b, preferred_element_type=f32)


def middle(work, x8, kernel, lanes):
    together = 4 * Z // lanes
    for block in range(0, Y // 8, together):
        groups = [slice(at * 8, at * 8 + 8) for at in range(block, block + together)]
        field = jnp.concatenate([work[:, g, :].reshape(X * 8, lanes) for g in groups], axis=1)
        scale = [kernel[:, g, :].reshape(X * 8, 2 * Z) for g in groups]
        scale = jnp.concatenate([t for t in scale for _ in range(lanes // (2 * Z))], axis=1)
        field = dot(x8[...], field.astype(bf16))
        field = dot(x8[...], (field * scale).astype(bf16))
        for at, g in enumerate(groups):
            work[:, g, :] = field[:, at * lanes : (at + 1) * lanes].reshape(X, 8, lanes)


def chunk(step, high, base=0):
    return pl.ds(pl.multiple_of(step * high + base, high), high)


def inward(trial, partner, z, y_in):
    trial = spread_rows(trial, trial)
    parts = [trial * partner[:, at : at + 2 * Z] for at in range(0, partner.shape[1], 2 * Z)]
    field = dot(jnp.concatenate(parts, axis=1), z).astype(bf16)
    return dot(y_in[...], field).reshape(XB, Y, partner.shape[1])


def outward(field, partner, z, y_out):
    field = field.reshape(ROWS, partner.shape[1]).astype(bf16)
    field = dot(dot(y_out[...], field).astype(bf16), z) * partner.astype(f32)
    return gather_rows(sum(field[:, at : at + 2 * Z] for at in range(0, field.shape[1], 2 * Z)))


def own_kernel(t_ref, p_ref, joined, kernel, o_ref, mine, work):
    z4, x8, y_in, y_out = views(joined)
    high = XB * HALF
    halves = [slice(0, 2 * Z), slice(2 * Z, 4 * Z)]
    for step in range(0, GROUPS, 2):
        density = []
        for at in (step, step + 1):
            rows, rows2 = chunk(at, high), chunk(at, high, X * HALF)
            partner = spread_rows(p_ref[rows, :], p_ref[rows2, :])
            mine[chunk(at, ROWS), :] = partner
            density.append(spread_rows(t_ref[rows, :], t_ref[rows, :]) * partner)
        field = dot(jnp.concatenate(density, axis=1), z4[...]).astype(bf16)
        field = dot(y_in[...], field)
        for at, lanes in zip((step, step + 1), halves):
            work[pl.ds(at * XB, XB)] = field[:, lanes].reshape(XB, Y, 2 * Z)
    middle(work, x8, kernel, 2 * Z)
    for step in range(0, GROUPS, 2):
        field = [work[pl.ds(at * XB, XB)].reshape(ROWS, 2 * Z) for at in (step, step + 1)]
        field = jnp.concatenate(field, axis=1).astype(bf16)
        field = dot(dot(y_out[...], field).astype(bf16), z4[...])
        for at, lanes in zip((step, step + 1), halves):
            partner = mine[chunk(at, ROWS), :].astype(f32)
            o_ref[pl.ds(at * XB, XB)] = gather_rows(field[:, lanes] * partner)


def cross_kernel(r_ref, t_ref, c_ref, q_ref, mine, own_ref, joined, kernel, o_ref, work, pairs):
    z4, x8, y_in, y_out = views(joined)
    block = lax.axis_index("orb")
    half = lax.axis_size("orb") // 2
    even = block % 2 == 0
    border = block % half >= half - 2
    high = XB * HALF
    for step in range(GROUPS):
        rows, rows2 = chunk(step, high), chunk(step, high, X * HALF)
        trial = jnp.where(even, r_ref[rows, :].astype(f32), t_ref[rows, :].astype(f32))
        carried = spread_rows(c_ref[rows, :], c_ref[rows2, :]).astype(f32)
        first = jnp.where(even, mine[chunk(step, ROWS), :].astype(f32), carried).astype(bf16)
        second = spread_rows(q_ref[rows, :], q_ref[rows2, :])
        partner = jnp.concatenate([first, second], axis=1)
        pairs[chunk(step, ROWS), :] = partner
        work[pl.ds(step * XB, XB)] = inward(trial, partner, z4[...], y_in)
    middle(work, x8, kernel, 4 * Z)
    for step in range(GROUPS):
        planes = pl.ds(step * XB, XB)
        cross = outward(work[planes], pairs[chunk(step, ROWS), :], z4[...], y_out)
        own = own_ref[planes] + jnp.where(even, 0.0, cross)
        turned = jnp.concatenate([cross[i : i + 1] for i in reversed(range(XB))], axis=0)
        cross = jnp.where(border, turned, cross)
        o_ref[planes] = jnp.concatenate([own, cross], axis=1).astype(bf16)


def rows_kernel(x_ref, o_ref):
    o_ref[...] = x_ref[...].reshape(o_ref.shape)


VMEM = pl.BlockSpec(memory_space=pltpu.VMEM)
GRANT = pltpu.CompilerParams(vmem_limit_bytes=16 * 2**20)


def as_rows(fields):
    return pl.pallas_call(
        rows_kernel,
        out_shape=jax.ShapeDtypeStruct((fields.shape[0] * X * HALF, 2 * Z), bf16),
        in_specs=[VMEM],
        out_specs=VMEM,
        cost_estimate=pl.CostEstimate(flops=0, bytes_accessed=10**6, transcendentals=0),
        compiler_params=GRANT,
        name="as_rows",
    )(fields)


COST = pl.CostEstimate(flops=4 * 10**9, bytes_accessed=3 * 10**6, transcendentals=0)


def own_call(trial, partner, tabs):
    return pl.pallas_call(
        own_kernel,
        out_shape=(
            jax.ShapeDtypeStruct((X, HALF, 2 * Z), f32),
            jax.ShapeDtypeStruct((X * Y, 2 * Z), bf16),
        ),
        in_specs=[VMEM] * 4,
        out_specs=(VMEM, VMEM),
        scratch_shapes=[pltpu.VMEM((X, Y, 2 * Z), f32)],
        cost_estimate=COST,
        compiler_params=GRANT,
        name="own_terms",
    )(trial, partner, *tabs)


def cross_call(remote, trial, carried, other, mine, own, tabs):
    return pl.pallas_call(
        cross_kernel,
        out_shape=jax.ShapeDtypeStruct((X, Y, 2 * Z), bf16),
        in_specs=[VMEM] * 8,
        out_specs=VMEM,
        scratch_shapes=[pltpu.VMEM((X, Y, 4 * Z), f32), pltpu.VMEM((X * Y, 4 * Z), bf16)],
        cost_estimate=COST,
        compiler_params=GRANT,
        name="cross_terms",
    )(remote, trial, carried, other, mine, own, *tabs)


def route(blocks, groups, distance, parity, turn):
    half = blocks // 2
    pairs = []
    for block in range(parity, blocks, 2):
        target = (block + distance) % blocks
        for group in range(groups):
            place = group ^ turn if target // half != block // half else group
            pairs.append((block * groups + group, target * groups + place))
    return pairs


def local(targets, partners):
    blocks, groups = lax.axis_size("orb"), lax.axis_size("grp")
    send = lambda what, *how: lax.ppermute(what, ("orb", "grp"), route(blocks, groups, *how))
    tabs = tables()
    target = as_rows(targets)
    remote = send(target, -2, 0, 3)
    partner = as_rows(partners)
    carried = send(partner, 2, 1, 2)
    other = lax.ppermute(partner, "orb", [(i ^ 1, i) for i in range(blocks)])
    own, mine = own_call(target, partner, tabs)
    fields = cross_call(remote, target, carried, other, mine, own, tabs)
    slabs = lax.all_to_all(fields, "grp", 0, 0, tiled=True)
    summed = jnp.sum(slabs.astype(f32), axis=0)
    ahead = send(summed[HALF:], 2, 0, 3)
    factor = -1.0 / math.sqrt(STEPS * groups * 2)
    return ((summed[:HALF] + ahead) * factor).reshape(1, Y * Z)


def solution(mesh):
    in_specs = (P("orb", None), P(("orb", "grp"), None))
    out_specs = P("orb", "grp")
    return jax.shard_map(local, mesh=mesh, in_specs=in_specs, out_specs=out_specs, check_vma=False)
```
